256 devices in a mesh: pairs: 64 (over z, x, core), rep: 4 (over y).
Axes of the slice: x: 4, y: 4, z: 8, core: 2. Of those that a mesh axis runs over, the one named last changes fastest.
Arguments:
- factors: bfloat16 [64, 512, 512], P('pairs', 'rep'), may hold values from -1.1953125 to 1.1953125
- orbital_virtuals: bfloat16 [64, 512, 128], P('pairs'), may hold values from -0.25 to 0.25
- occupied: bfloat16 [64], P('pairs'), may hold values from -1.5 to -0.29882812
- pair_rotations: bfloat16 [2048, 2, 128, 128], P('pairs'), may hold values from -0.5 to 0.5
- pair_energies: float32 [2048, 2, 128], P('pairs'), may hold values from 0.5 to 4
- pair_orbitals: int32 [2048, 2], P('pairs'), may hold values from 0 to 63
- pair_ranks: int32 [2048], P('pairs'), may hold values from 32 to 128
- margins: bfloat16 [2048, 6, 128, 128], P('pairs'), may hold values from -0.5 to 0.5
- coupling_weight: float32 [2048, 6], P('pairs'), may hold values from -4 to 4
- send_slots: int32 [64, 64, 2], P('pairs'), may hold values from 0 to 31
- couplings: int32 [2048, 6], P('pairs'), may hold values from 0 to 127
Outputs:
- amplitudes: bfloat16 [2048, 128, 128], P('pairs')
- densities: float32 [64, 128, 128], P('pairs')
The draws below stay inside these ranges and needn't reach their ends.
Inputs may be any that keep to these rules, and one draw needn't show every extreme that they name: `pair_orbitals`: the first and second orbital of a pair; they may be equal. `pair_ranks`: positions at or past a pair's rank are padding. send_slots[q, d, s] is the local pair, on index q of pairs, whose amplitudes fill slot s of what q sends to index d. `couplings`: entry k of a pair on index d names slot k % 2 of what index k // 2 sends to d.
All inputs are finite; a program needn't handle non-finite values.
Results may differ from the reference program's by a relative error of at most 0.0085.
Values may be sent and summed in bfloat16 or wider, within the bound.
No kernel may reach another device: no remote copies, remote signals or barrier semaphores. Data moves between devices by JAX's collectives and lax.ppermute only.
A program may use at most 64 MiB of HBM per device.

```python
import math
import jax
import jax.numpy as jnp
from jax import lax

NAUX = 512
NPAO = 512
RANK = 128
PAIR_DEV = 32
NCOUP = 6
CAPA = 2
ITERS = 3
OWNERS = 64
NORB = 64
NPAIR = 2048


def plant(drawn, key, least, top_value):
    index_at = [jax.random.randint(jax.random.fold_in(key, axis), (), 0, length) for axis, length in enumerate(drawn.shape)]
    widest = drawn.shape.index(max(drawn.shape))
    next_to = index_at[:widest] + [(index_at[widest] + 1) % drawn.shape[widest]] + index_at[widest + 1:]
    return drawn.at[tuple(index_at)].set(least).at[tuple(next_to)].set(top_value)


def levels(key, extent, cuts, low, largest):
    loudness, own = 1.0, jax.random.fold_in(key, 6)
    for position, parts in cuts:
        heights = jnp.exp(jax.random.uniform(jax.random.fold_in(own, position), (parts,), jnp.float32, low / len(cuts), largest / len(cuts)))
        loudness = loudness * jnp.repeat(heights, extent[position] // parts).reshape([-1 if axis == position else 1 for axis in range(len(extent))])
    return loudness


def gaussian(rng, shape, spread, bound, pieces=(), held_as=jnp.bfloat16):
    gain = levels(rng, shape, pieces, -0.22, 0.18) if pieces else 1.0
    drawn = jax.random.normal(rng, shape, jnp.float32) * spread * gain
    return jnp.minimum(jnp.maximum(drawn, -bound), bound).astype(held_as)


def setup_inputs(seed: int = 0) -> dict:
    splits = jax.random.split(jax.random.key(seed), 12)
    factors = gaussian(splits[0], (NORB, NAUX, NPAO), 0.2, 1.1953125, ((0, 64), (1, 4)))
    orbital_virtuals = gaussian(splits[1], (NORB, NPAO, RANK), NPAO ** -0.5, 0.25, ((0, 64),))
    occupied = jnp.clip(-1.5 + 1.2011719 * jax.random.uniform(splits[2], (NORB,), jnp.float32) ** levels(splits[2], (NORB,), ((0, 64),), -0.2, 0.2), -1.5, -0.29882812).astype(jnp.bfloat16)
    pair_rotations = gaussian(splits[3], (NPAIR, 2, RANK, RANK), RANK ** -0.5, 0.5, ((0, 64),))
    pair_energies = jnp.clip(jnp.exp(math.log(4.0) - 2.0794415 * jax.random.uniform(splits[4], (NPAIR, 2, RANK), jnp.float32) ** levels(splits[4], (NPAIR, 2, RANK), ((0, 64),), -0.2, 0.2)), 0.5, 4.0)
    pair_orbitals = plant(jax.random.randint(splits[5], (NPAIR, 2), 0, NORB), jax.random.fold_in(splits[5], 1), 0, NORB - 1).astype(jnp.int32)
    pair_ranks = plant(jax.random.randint(splits[6], (NPAIR,), RANK // 4, RANK + 1), jax.random.fold_in(splits[6], 1), RANK // 4, RANK).astype(jnp.int32)
    margins = gaussian(splits[7], (NPAIR, NCOUP, RANK, RANK), RANK ** -0.5, 0.5, ((0, 64),))
    coupling_weight = jnp.clip(jax.random.uniform(splits[8], (NPAIR, NCOUP), jnp.float32, -4.0, 4.0) * levels(splits[8], (NPAIR, NCOUP), ((0, 64),), -0.4, 0.0), -4.0, 4.0)
    send_slots = plant(jax.random.randint(splits[9], (OWNERS, OWNERS, CAPA), 0, PAIR_DEV), jax.random.fold_in(splits[9], 1), 0, PAIR_DEV - 1).astype(jnp.int32)
    couplings = plant(jax.random.randint(splits[10], (NPAIR, NCOUP), 0, OWNERS * CAPA), jax.random.fold_in(splits[10], 1), 0, (OWNERS * CAPA) - 1).astype(jnp.int32)
    return dict(factors=factors, orbital_virtuals=orbital_virtuals, occupied=occupied, pair_rotations=pair_rotations, pair_energies=pair_energies, pair_orbitals=pair_orbitals, pair_ranks=pair_ranks, margins=margins, coupling_weight=coupling_weight, send_slots=send_slots, couplings=couplings)


def reference(factors, orbital_virtuals, occupied, pair_rotations, pair_energies, pair_orbitals, pair_ranks, margins, coupling_weight, send_slots, couplings):
    halves = jnp.einsum("oxp,opr->oxr", factors.astype(jnp.float32), orbital_virtuals.astype(jnp.float32), precision=lax.Precision.HIGHEST).astype(jnp.bfloat16)
    rank_size = pair_rotations.shape[-1]
    positions = jnp.arange(rank_size, dtype=jnp.int32)
    visible = (positions[None, :] < pair_ranks[:, None]).astype(jnp.float32)
    mask_pair = visible[:, :, None] * visible[:, None, :]
    occ_pair = occupied[pair_orbitals[:, 0]].astype(jnp.float32) + occupied[pair_orbitals[:, 1]].astype(jnp.float32)
    denominator = pair_energies[:, 0, :, None] + pair_energies[:, 1, None, :] - occ_pair[:, None, None]

    def integral_block(block_index):
        first_row = (block_index * PAIR_DEV).astype(jnp.int32)
        orbital_rows = lax.dynamic_slice_in_dim(pair_orbitals, first_row, PAIR_DEV, 0)
        rotations = lax.dynamic_slice_in_dim(pair_rotations, first_row, PAIR_DEV, 0).astype(jnp.float32)
        left_half = halves[orbital_rows[:, 0]].astype(jnp.float32)
        right_half = halves[orbital_rows[:, 1]].astype(jnp.float32)
        mixed_pair = jnp.einsum("pxa,pxb->pab", left_half, right_half, precision=lax.Precision.HIGHEST)
        half_turn = jnp.einsum("pxa,pxy->pay", rotations[:, 0], mixed_pair, precision=lax.Precision.HIGHEST)
        return jnp.einsum("pay,pyb->pab", half_turn, rotations[:, 1], precision=lax.Precision.HIGHEST)

    block_ids = jnp.arange(OWNERS, dtype=jnp.int32)
    integral = lax.map(integral_block, block_ids).reshape(NPAIR, rank_size, rank_size) * mask_pair
    device_index = jnp.arange(NPAIR, dtype=jnp.int32) // PAIR_DEV
    source = couplings // CAPA
    slot_index = couplings % CAPA
    partner = source * PAIR_DEV + send_slots[source, device_index[:, None], slot_index]
    amplitude = (-integral / denominator).astype(jnp.bfloat16)
    for iteration in range(ITERS):
        def relax_block(block_index, current=amplitude):
            first_row = (block_index * PAIR_DEV).astype(jnp.int32)
            links = lax.dynamic_slice_in_dim(partner, first_row, PAIR_DEV, 0)
            partner_amp = current[links].astype(jnp.float32)
            margin_rows = lax.dynamic_slice_in_dim(margins, first_row, PAIR_DEV, 0).astype(jnp.float32)
            left_turn = jnp.einsum("pcab,pcbd->pcad", margin_rows, partner_amp, precision=lax.Precision.HIGHEST).astype(jnp.bfloat16)
            left_turn = lax.optimization_barrier(left_turn).astype(jnp.float32)
            transformed = jnp.einsum("pcad,pced->pcae", left_turn, margin_rows, precision=lax.Precision.HIGHEST)
            weight = lax.dynamic_slice_in_dim(coupling_weight, first_row, PAIR_DEV, 0)
            coupled = jnp.einsum("pc,pcae->pae", weight, transformed, precision=lax.Precision.HIGHEST)
            integral_rows = lax.dynamic_slice_in_dim(integral, first_row, PAIR_DEV, 0)
            denominator_rows = lax.dynamic_slice_in_dim(denominator, first_row, PAIR_DEV, 0)
            mask_rows = lax.dynamic_slice_in_dim(mask_pair, first_row, PAIR_DEV, 0)
            return (-(integral_rows - coupled) / denominator_rows * mask_rows).astype(jnp.bfloat16)

        amplitude = lax.map(relax_block, block_ids).reshape(NPAIR, rank_size, rank_size)
    rotations = pair_rotations.astype(jnp.float32)
    amplitude_wide = amplitude.astype(jnp.float32)
    side_left = jnp.einsum("pxa,pab->pxb", rotations[:, 0], amplitude_wide, precision=lax.Precision.HIGHEST).astype(jnp.bfloat16)
    side_right = jnp.einsum("pyb,pab->pya", rotations[:, 1], amplitude_wide, precision=lax.Precision.HIGHEST).astype(jnp.bfloat16)
    side_left = lax.optimization_barrier(side_left).astype(jnp.float32)
    side_right = lax.optimization_barrier(side_right).astype(jnp.float32)
    gram_left = jnp.einsum("pxb,pzb->pxz", side_left, side_left, precision=lax.Precision.HIGHEST)
    gram_right = jnp.einsum("pxb,pzb->pxz", side_right, side_right, precision=lax.Precision.HIGHEST)
    densities = jax.ops.segment_sum(gram_left, pair_orbitals[:, 0], NORB) + jax.ops.segment_sum(gram_right, pair_orbitals[:, 1], NORB)
    return amplitude, densities / rank_size
```

```python
import jax
import jax.numpy as jnp
from jax import lax
from jax.experimental import pallas as pl
from jax.experimental.pallas import tpu as pltpu
from jax.sharding import Mesh
from jax.sharding import PartitionSpec as P

ITERS = 3
PAIRS = ("pairs_0", "pairs_1", "pairs_2")
PLANE = ("pairs_0", "pairs_1")
REP = 4
STEP = 4
F32, BF16 = jnp.float32, jnp.bfloat16
NN = (((1,), (0,)), ((), ()))
NT = (((1,), (1,)), ((), ()))
TN = (((0,), (0,)), ((), ()))


def mm(a, b, dims):
    return lax.dot_general(a, b, dims, preferred_element_type=F32)


def shift(x, axis, count, by):
    return lax.ppermute(x, axis, [(i, (i + by) % count) for i in range(count)])


def store_shares(total, share_ref, rank_at, outs, at):
    share_ref[at] = total
    for k, out in enumerate(outs):
        first = pl.multiple_of(lax.rem(rank_at + k, REP) * 32, 32)
        out[at] = share_ref[at, pl.ds(first, 32), :].astype(out.dtype)


def integral_kernel(idx, *refs):
    pieces, (rot, o0, o1, o2, o3, occ, held, share) = refs[:8], refs[8:]
    step = pl.program_id(0)

    @pl.when(step == 0)
    def _():
        for i, piece in enumerate(pieces):
            held[8 * i : 8 * i + 8] = piece[...]

    for n in range(STEP):
        i, j = idx[1 + step * STEP + n], idx[33 + step * STEP + n]
        left = mm(held[i, :128, :], rot[n, 0], NN)
        right = mm(held[j, :128, :], rot[n, 1], NN)
        left_hi, right_hi = left.astype(BF16), right.astype(BF16)
        left_lo = (left - left_hi.astype(F32)).astype(BF16)
        right_lo = (right - right_hi.astype(F32)).astype(BF16)
        total = mm(
            jnp.concatenate([right_hi, right_hi, right_lo], 0),
            jnp.concatenate([left_hi, left_lo, left_hi], 0),
            TN,
        )
        store_shares(total, share, idx[0], (o0, o1, o2, o3), n)
        occ[n] = held[i, 128:144, :].astype(F32)[:1] + held[j, 128:144, :].astype(F32)[:1]


def visible_rows(idx, p, first):
    rank = idx[1 + p]
    b = lax.broadcasted_iota(jnp.int32, (32, 128), 0) + first
    a = lax.broadcasted_iota(jnp.int32, (32, 128), 1)
    return (b < rank) & (a < rank)


def start_kernel(idx, own, r1, r2, r3, energy, occ, integral, denominator, amplitude):
    first = idx[0] * 32

    def one(p, carry):
        total = own[p] + r1[p].astype(F32) + r2[p].astype(F32) + r3[p].astype(F32)
        value = jnp.where(visible_rows(idx, p, first), total, 0.0)
        denom = energy[p] - occ[p]
        integral[p] = value
        denominator[p] = denom
        amplitude[p] = (-value / denom).astype(BF16)
        return carry

    lax.fori_loop(0, 32, one, 0, unroll=4)


def update_kernel(idx, own, r1, r2, r3, integral, denominator, amplitude):
    first = idx[0] * 32

    def one(p, carry):
        coupled = own[p] + r1[p].astype(F32) + r2[p].astype(F32) + r3[p].astype(F32)
        value = -(integral[p] - coupled) / denominator[p]
        amplitude[p] = jnp.where(visible_rows(idx, p, first), value, 0.0).astype(BF16)
        return carry

    lax.fori_loop(0, 32, one, 0, unroll=4)


def outgoing_kernel(idx, own, other, out):
    def one(d, carry):
        for s in range(2):
            out[d * 4 + s] = own[idx[d * 4 + s]]
            out[d * 4 + 2 + s] = other[idx[d * 4 + 2 + s]]
        return carry

    lax.fori_loop(0, 32, one, 0, unroll=4)


def columns_kernel(idx, margin, out):
    k = lax.broadcasted_iota(jnp.int32, (128, 192), 0)
    col = lax.broadcasted_iota(jnp.int32, (128, 192), 1)
    for n in range(STEP):
        total = jnp.zeros((128, 192), F32)
        for c in range(6):
            chosen = (col - 32 * c + 32 * idx[0] == k) & (col >= 32 * c) & (col < 32 * c + 32)
            total += mm(margin[n, c], chosen.astype(F32).astype(BF16), NN)
        out[n] = total.astype(BF16)


def relax_kernel(idx, weight, arrived, margin, columns, o0, o1, o2, o3, lefts, share):
    step = pl.program_id(0)
    for n in range(STEP):
        for c in range(6):
            at = (step * STEP + n) * 6 + c
            left = mm(arrived[idx[1 + at]], margin[n, c], NT)
            lefts[n, 32 * c : 32 * c + 32, :] = (left * weight[at]).astype(BF16)
        total = mm(columns[n], lefts[n], NN)
        store_shares(total, share, idx[0], (o0, o1, o2, o3), n)


def density_kernel(idx, t0, t1, t2, t3, rot, amplitude, d0, d1, whole, sides, grams, acc):
    step = pl.program_id(0)

    @pl.when(step == 0)
    def _():
        acc[...] = jnp.zeros_like(acc)

    mine = pl.multiple_of(idx[0] * 32, 32)
    for n in range(STEP):
        for k, piece in enumerate((t0, t1, t2, t3)):
            first = pl.multiple_of(lax.rem(idx[0] + REP - k, REP) * 32, 32)
            whole[n, pl.ds(first, 32), :] = piece[n]
        amp_t = whole[n]
        amplitude[n] = amp_t.T
        side = mm(rot[n, 0], amp_t, NT).astype(BF16)
        sides[2 * n] = side
        grams[2 * n] = mm(sides[2 * n, pl.ds(mine, 32), :], side, NT)
        side = mm(rot[n, 1], amp_t, NN).astype(BF16)
        sides[2 * n + 1] = side
        grams[2 * n + 1] = mm(sides[2 * n + 1, pl.ds(mine, 32), :], side, NT)

    def add(k, carry):
        at = idx[1 + step * 2 * STEP + k]
        acc[at] = acc[at] + grams[k]
        return carry

    lax.fori_loop(0, 2 * STEP, add, 0)

    @pl.when(step == pl.num_programs(0) - 1)
    def _():
        d0[...] = acc[:32]
        d1[...] = acc[32:]


def whole_spec(shape):
    return pl.BlockSpec(shape, lambda g, *_: (0,) * len(shape))


def step_spec(shape):
    return pl.BlockSpec((STEP, *shape), lambda g, *_: (g,) + (0,) * len(shape))


def call(kernel, scalars, args, in_specs, outs, out_specs, scratch=(), grid=(8,), cost=None):
    return pl.pallas_call(
        kernel,
        grid_spec=pltpu.PrefetchScalarGridSpec(
            num_scalar_prefetch=len(scalars),
            grid=grid,
            in_specs=in_specs,
            out_specs=out_specs,
            scratch_shapes=list(scratch),
        ),
        out_shape=outs,
        cost_estimate=cost,
    )(*scalars, *args)


def struct(shape, dtype):
    return jax.ShapeDtypeStruct(shape, dtype)


def summed_over_rep(shares):
    return (shares[0],) + tuple(shift(shares[k], "rep", REP, k) for k in (1, 2, 3))


def body(
    factors,
    orbital_virtuals,
    occupied,
    pair_rotations,
    pair_energies,
    pair_orbitals,
    pair_ranks,
    margins,
    coupling_weight,
    send_slots,
    couplings,
):
    core, rep, col = lax.axis_index("pairs_2"), lax.axis_index("rep"), lax.axis_index("pairs_1")
    rep1 = rep[None].astype(jnp.int32)
    share3 = (32, 32, 128)
    share_structs = [struct(share3, F32)] + [struct(share3, BF16)] * 3
    share_specs = [step_spec((32, 128))] * 4
    share_scratch = pltpu.VMEM((STEP, 128, 128), F32)

    halves = mm(factors[0], orbital_virtuals[0], NN).astype(BF16)
    sent = jnp.concatenate([halves, jnp.broadcast_to(occupied[:, None], (16, 128))], 0)
    along_z = lax.all_to_all(
        jnp.broadcast_to(sent[None], (8, 144, 128)), "pairs_0", 0, 0, tiled=True
    )
    pieces = [along_z] + [shift(along_z, "pairs_1", 4, k) for k in (1, 2, 3)]
    pieces += [shift(piece, "pairs_2", 2, 1) for piece in pieces]

    orb = pair_orbitals
    orb_z, orb_x, orb_c = orb // 8, (orb // 2) % 4, orb % 2
    held_at = (((orb_c ^ core) * 4 + (col - orb_x) % 4) * 8 + orb_z).T.reshape(-1)
    o0, o1, o2, o3, occ = call(
        integral_kernel,
        [jnp.concatenate([rep1, held_at])],
        [*pieces, pair_rotations],
        [whole_spec((8, 144, 128))] * 8 + [step_spec((2, 128, 128))],
        share_structs + [struct((32, 1, 128), F32)],
        share_specs + [step_spec((1, 128))],
        [pltpu.VMEM((64, 144, 128), BF16), share_scratch],
    )

    (columns,) = call(
        columns_kernel,
        [rep1],
        [margins],
        [step_spec((6, 128, 128))],
        [struct((32, 128, 192), BF16)],
        [step_spec((128, 192))],
        cost=pl.CostEstimate(
            flops=32 * 6 * 2 * 128 * 128 * 192, bytes_accessed=9 << 20, transcendentals=0
        ),
    )
    energy_col = lax.dynamic_slice_in_dim(pair_energies[:, 1], rep * 32, 32, 1)
    energy = energy_col[:, :, None] + pair_energies[:, 0][:, None, :]
    ranks = jnp.concatenate([rep1, pair_ranks])
    other_slots = shift(send_slots, "pairs_2", 2, 1)
    slots = jnp.concatenate(
        [lax.dynamic_index_in_dim(s.reshape(32, 2, 2), core, 1) for s in (send_slots, other_slots)],
        1,
    ).reshape(-1)
    owner = couplings // 2
    arrived_at = (owner // 2) * 4 + ((owner % 2) ^ core) * 2 + couplings % 2
    links = jnp.concatenate([rep1, arrived_at.reshape(-1)])
    weights = coupling_weight.reshape(-1)
    share_in = [whole_spec(share3)]

    integral, denominator, amplitude = call(
        start_kernel,
        [ranks],
        [*summed_over_rep((o0, o1, o2, o3)), energy, occ],
        share_in * 5 + [whole_spec((32, 1, 128))],
        [struct(share3, F32), struct(share3, F32), struct(share3, BF16)],
        share_in * 3,
        grid=(1,),
    )
    for _ in range(ITERS):
        (outgoing,) = call(
            outgoing_kernel,
            [slots],
            [amplitude, shift(amplitude, "pairs_2", 2, 1)],
            share_in * 2,
            [struct((128, 32, 128), BF16)],
            [whole_spec((128, 32, 128))],
            grid=(1,),
        )
        arrived = lax.all_to_all(outgoing, PLANE, 0, 0, tiled=True)
        shares = call(
            relax_kernel,
            [links, weights],
            [arrived, margins, columns],
            [whole_spec((128, 32, 128)), step_spec((6, 128, 128)), step_spec((128, 192))],
            share_structs,
            share_specs,
            [pltpu.VMEM((STEP, 192, 128), BF16), share_scratch],
        )
        (amplitude,) = call(
            update_kernel,
            [ranks],
            [*summed_over_rep(shares), integral, denominator],
            share_in * 6,
            [struct(share3, BF16)],
            share_in,
            grid=(1,),
        )

    parts = [amplitude] + [shift(amplitude, "rep", REP, k) for k in (1, 2, 3)]
    dense_at = ((orb_c ^ core) * 32 + orb // 2).reshape(-1)
    final, d_own, d_other = call(
        density_kernel,
        [jnp.concatenate([rep1, dense_at])],
        [*parts, pair_rotations],
        share_specs + [step_spec((2, 128, 128))],
        [struct((32, 128, 128), BF16), struct(share3, F32), struct(share3, F32)],
        [step_spec((128, 128))] + share_in * 2,
        [
            pltpu.VMEM((STEP, 128, 128), BF16),
            pltpu.VMEM((2 * STEP, 128, 128), BF16),
            pltpu.VMEM((2 * STEP, 32, 128), F32),
            pltpu.VMEM((64, 32, 128), F32),
        ],
    )
    both = (d_own + shift(d_other, "pairs_2", 2, 1)).astype(BF16)
    arrived = lax.all_to_all(both, PLANE, 0, 0, tiled=True)
    mine = jnp.sum(arrived.astype(F32), 0) / 128
    rows = jnp.stack([mine] + [shift(mine, "rep", REP, k) for k in (1, 2, 3)])
    order = (rep - jnp.arange(REP, dtype=jnp.int32)) % REP
    densities = jnp.take(rows, order, axis=0).reshape(1, 128, 128)
    return (final, densities)


def solution(mesh):
    finer = Mesh(
        mesh.devices.reshape(8, 4, 2, mesh.shape["rep"]), ("pairs_0", "pairs_1", "pairs_2", "rep")
    )
    return jax.shard_map(
        body,
        mesh=finer,
        in_specs=(
            P(PAIRS, "rep", None),
            P(PAIRS, None, None),
            P(PAIRS),
            P(PAIRS, None, None, None),
            P(PAIRS, None, None),
            P(PAIRS, None),
            P(PAIRS),
            P(PAIRS, None, None, None),
            P(PAIRS, None),
            P(PAIRS, None, None),
            P(PAIRS, None),
        ),
        out_specs=(P(PAIRS, None, None), P(PAIRS, None, None)),
        check_vma=False,
    )
```

```python
import jax
import jax.numpy as jnp
from jax import lax
from jax.experimental import pallas as pl
from jax.experimental.pallas import tpu as pltpu
from jax.sharding import Mesh
from jax.sharding import PartitionSpec as P

ITERS = 3
PAIRS = ("pairs_0", "pairs_1", "pairs_2")
PLANE = ("pairs_0", "pairs_1")
REP = 4
STEP = 4
LIMIT = 12 << 20
F32, BF16 = jnp.float32, jnp.bfloat16
NN = (((1,), (0,)), ((), ()))
NT = (((1,), (1,)), ((), ()))
TN = (((0,), (0,)), ((), ()))


def mm(a, b, dims):
    return lax.dot_general(a, b, dims, preferred_element_type=F32)


def shift(x, axis, count, by):
    return lax.ppermute(x, axis, [(i, (i + by) % count) for i in range(count)])


def store_shares(total, share_ref, n, rank_at, outs, at):
    share_ref[n] = total
    for k, out in enumerate(outs):
        first = pl.multiple_of(lax.rem(rank_at + k, REP) * 32, 32)
        out[at] = share_ref[n, pl.ds(first, 32), :].astype(out.dtype)


def each_step(body_of):
    def one(step, carry):
        body_of(step)
        return carry

    lax.fori_loop(0, 32 // STEP, one, 0)


def integral_kernel(idx, *refs):
    pieces, (rot, o0, o1, o2, o3, occ, held, share) = refs[:8], refs[8:]
    for i, piece in enumerate(pieces):
        held[8 * i : 8 * i + 8] = piece[...]

    def some(step):
        for n in range(STEP):
            p = step * STEP + n
            i, j = idx[1 + p], idx[33 + p]
            left = mm(held[i, :128, :], rot[p, 0], NN)
            right = mm(held[j, :128, :], rot[p, 1], NN)
            left_hi, right_hi = left.astype(BF16), right.astype(BF16)
            left_lo = (left - left_hi.astype(F32)).astype(BF16)
            right_lo = (right - right_hi.astype(F32)).astype(BF16)
            total = mm(
                jnp.concatenate([right_hi, right_hi, right_lo], 0),
                jnp.concatenate([left_hi, left_lo, left_hi], 0),
                TN,
            )
            store_shares(total, share, n, idx[0], (o0, o1, o2, o3), p)
            occ[p] = held[i, 128:144, :].astype(F32)[:1] + held[j, 128:144, :].astype(F32)[:1]

    each_step(some)


def visible_rows(idx, p, first):
    rank = idx[1 + p]
    b = lax.broadcasted_iota(jnp.int32, (32, 128), 0) + first
    a = lax.broadcasted_iota(jnp.int32, (32, 128), 1)
    return (b < rank) & (a < rank)


def start_kernel(idx, own, r1, r2, r3, energy, occ, integral, denominator, amplitude):
    first = idx[0] * 32

    def one(p, carry):
        total = own[p] + r1[p].astype(F32) + r2[p].astype(F32) + r3[p].astype(F32)
        value = jnp.where(visible_rows(idx, p, first), total, 0.0)
        denom = energy[p] - occ[p]
        integral[p] = value
        denominator[p] = denom
        amplitude[p] = (-value / denom).astype(BF16)
        return carry

    lax.fori_loop(0, 32, one, 0, unroll=4)


def update_kernel(idx, own, r1, r2, r3, integral, denominator, amplitude):
    first = idx[0] * 32

    def one(p, carry):
        coupled = own[p] + r1[p].astype(F32) + r2[p].astype(F32) + r3[p].astype(F32)
        value = -(integral[p] - coupled) / denominator[p]
        amplitude[p] = jnp.where(visible_rows(idx, p, first), value, 0.0).astype(BF16)
        return carry

    lax.fori_loop(0, 32, one, 0, unroll=4)


def outgoing_kernel(idx, own, other, out):
    def one(d, carry):
        for s in range(2):
            out[d * 4 + s] = own[idx[d * 4 + s]]
            out[d * 4 + 2 + s] = other[idx[d * 4 + 2 + s]]
        return carry

    lax.fori_loop(0, 32, one, 0, unroll=4)


def columns_kernel(idx, margin, turned, out, rows):
    mine = pl.multiple_of(idx[0] * 32, 32)

    def some(step):
        for n in range(STEP):
            p = step * STEP + n
            for c in range(6):
                turned[p, c] = margin[p, c].T
                rows[n, 32 * c : 32 * c + 32, :] = turned[p, c, pl.ds(mine, 32), :]
            out[p] = rows[n].T

    each_step(some)


def relax_kernel(idx, weight, arrived, turned, columns, o0, o1, o2, o3, lefts, share):
    def some(step):
        for n in range(STEP):
            p = step * STEP + n
            for c in range(6):
                left = mm(arrived[idx[1 + p * 6 + c]], turned[p, c], NN)
                lefts[n, 32 * c : 32 * c + 32, :] = (left * weight[p * 6 + c]).astype(BF16)
            total = mm(columns[p], lefts[n], NN)
            store_shares(total, share, n, idx[0], (o0, o1, o2, o3), p)

    each_step(some)


def density_kernel(idx, t0, t1, t2, t3, rot, amplitude, d0, d1, whole, sides, grams, acc):
    acc[...] = jnp.zeros_like(acc)
    mine = pl.multiple_of(idx[0] * 32, 32)

    def some(step):
        for n in range(STEP):
            p = step * STEP + n
            for k, piece in enumerate((t0, t1, t2, t3)):
                first = pl.multiple_of(lax.rem(idx[0] + REP - k, REP) * 32, 32)
                whole[n, pl.ds(first, 32), :] = piece[p]
            amp_t = whole[n]
            amplitude[p] = amp_t.T
            side = mm(rot[p, 0], amp_t, NT).astype(BF16)
            sides[2 * n] = side
            grams[2 * n] = mm(sides[2 * n, pl.ds(mine, 32), :], side, NT)
            side = mm(rot[p, 1], amp_t, NN).astype(BF16)
            sides[2 * n + 1] = side
            grams[2 * n + 1] = mm(sides[2 * n + 1, pl.ds(mine, 32), :], side, NT)

        def add(k, carry):
            at = idx[1 + step * 2 * STEP + k]
            acc[at] = acc[at] + grams[k]
            return carry

        lax.fori_loop(0, 2 * STEP, add, 0)

    each_step(some)
    d0[...] = acc[:32]
    d1[...] = acc[32:]


def call(kernel, scalars, args, outs, scratch=(), cost=None):
    vmem, smem = pl.BlockSpec(memory_space=pltpu.VMEM), pl.BlockSpec(memory_space=pltpu.SMEM)
    return pl.pallas_call(
        kernel,
        in_specs=[smem] * len(scalars) + [vmem] * len(args),
        out_specs=[vmem] * len(outs),
        scratch_shapes=list(scratch),
        out_shape=outs,
        cost_estimate=cost,
        compiler_params=pltpu.CompilerParams(vmem_limit_bytes=LIMIT),
    )(*scalars, *args)


def struct(shape, dtype):
    return jax.ShapeDtypeStruct(shape, dtype)


def summed_over_rep(shares):
    return (shares[0],) + tuple(shift(shares[k], "rep", REP, k) for k in (1, 2, 3))


def body(
    factors,
    orbital_virtuals,
    occupied,
    pair_rotations,
    pair_energies,
    pair_orbitals,
    pair_ranks,
    margins,
    coupling_weight,
    send_slots,
    couplings,
):
    core, rep, col = lax.axis_index("pairs_2"), lax.axis_index("rep"), lax.axis_index("pairs_1")
    rep1 = rep[None].astype(jnp.int32)
    share3 = (32, 32, 128)
    share_structs = [struct(share3, F32)] + [struct(share3, BF16)] * 3
    share_scratch = pltpu.VMEM((STEP, 128, 128), F32)

    halves = mm(factors[0], orbital_virtuals[0], NN).astype(BF16)
    sent = jnp.concatenate([halves, jnp.broadcast_to(occupied[:, None], (16, 128))], 0)
    along_z = lax.all_to_all(
        jnp.broadcast_to(sent[None], (8, 144, 128)), "pairs_0", 0, 0, tiled=True
    )
    pieces = [along_z] + [shift(along_z, "pairs_1", 4, k) for k in (1, 2, 3)]
    pieces += [shift(piece, "pairs_2", 2, 1) for piece in pieces]

    orb = pair_orbitals
    orb_z, orb_x, orb_c = orb // 8, (orb // 2) % 4, orb % 2
    held_at = (((orb_c ^ core) * 4 + (col - orb_x) % 4) * 8 + orb_z).T.reshape(-1)
    o0, o1, o2, o3, occ = call(
        integral_kernel,
        [jnp.concatenate([rep1, held_at])],
        [*pieces, pair_rotations],
        share_structs + [struct((32, 1, 128), F32)],
        [pltpu.VMEM((64, 144, 128), BF16), share_scratch],
    )

    turned, columns = call(
        columns_kernel,
        [rep1],
        [margins],
        [struct((32, 6, 128, 128), BF16), struct((32, 128, 192), BF16)],
        [pltpu.VMEM((STEP, 192, 128), BF16)],
        cost=pl.CostEstimate(
            flops=32 * 6 * 2 * 128 * 128 * 192, bytes_accessed=9 << 20, transcendentals=0
        ),
    )
    energy_col = lax.dynamic_slice_in_dim(pair_energies[:, 1], rep * 32, 32, 1)
    energy = energy_col[:, :, None] + pair_energies[:, 0][:, None, :]
    ranks = jnp.concatenate([rep1, pair_ranks])
    other_slots = shift(send_slots, "pairs_2", 2, 1)
    slots = jnp.concatenate(
        [lax.dynamic_index_in_dim(s.reshape(32, 2, 2), core, 1) for s in (send_slots, other_slots)],
        1,
    ).reshape(-1)
    owner = couplings // 2
    arrived_at = (owner // 2) * 4 + ((owner % 2) ^ core) * 2 + couplings % 2
    links = jnp.concatenate([rep1, arrived_at.reshape(-1)])
    weights = coupling_weight.reshape(-1)

    integral, denominator, amplitude = call(
        start_kernel,
        [ranks],
        [*summed_over_rep((o0, o1, o2, o3)), energy, occ],
        [struct(share3, F32), struct(share3, F32), struct(share3, BF16)],
    )
    for _ in range(ITERS):
        (outgoing,) = call(
            outgoing_kernel,
            [slots],
            [amplitude, shift(amplitude, "pairs_2", 2, 1)],
            [struct((128, 32, 128), BF16)],
        )
        arrived = lax.all_to_all(outgoing, PLANE, 0, 0, tiled=True)
        shares = call(
            relax_kernel,
            [links, weights],
            [arrived, turned, columns],
            share_structs,
            [pltpu.VMEM((STEP, 192, 128), BF16), share_scratch],
        )
        (amplitude,) = call(
            update_kernel,
            [ranks],
            [*summed_over_rep(shares), integral, denominator],
            [struct(share3, BF16)],
        )

    parts = [amplitude] + [shift(amplitude, "rep", REP, k) for k in (1, 2, 3)]
    dense_at = ((orb_c ^ core) * 32 + orb // 2).reshape(-1)
    final, d_own, d_other = call(
        density_kernel,
        [jnp.concatenate([rep1, dense_at])],
        [*parts, pair_rotations],
        [struct((32, 128, 128), BF16), struct(share3, F32), struct(share3, F32)],
        [
            pltpu.VMEM((STEP, 128, 128), BF16),
            pltpu.VMEM((2 * STEP, 128, 128), BF16),
            pltpu.VMEM((2 * STEP, 32, 128), F32),
            pltpu.VMEM((64, 32, 128), F32),
        ],
    )
    both = (d_own + shift(d_other, "pairs_2", 2, 1)).astype(BF16)
    arrived = lax.all_to_all(both, PLANE, 0, 0, tiled=True)
    mine = jnp.sum(arrived.astype(F32), 0) / 128
    rows = jnp.stack([mine] + [shift(mine, "rep", REP, k) for k in (1, 2, 3)])
    order = (rep - jnp.arange(REP, dtype=jnp.int32)) % REP
    densities = jnp.take(rows, order, axis=0).reshape(1, 128, 128)
    return (final, densities)


def solution(mesh):
    finer = Mesh(
        mesh.devices.reshape(8, 4, 2, mesh.shape["rep"]), ("pairs_0", "pairs_1", "pairs_2", "rep")
    )
    return jax.shard_map(
        body,
        mesh=finer,
        in_specs=(
            P(PAIRS, "rep", None),
            P(PAIRS, None, None),
            P(PAIRS),
            P(PAIRS, None, None, None),
            P(PAIRS, None, None),
            P(PAIRS, None),
            P(PAIRS),
            P(PAIRS, None, None, None),
            P(PAIRS, None),
            P(PAIRS, None, None),
            P(PAIRS, None),
        ),
        out_specs=(P(PAIRS, None, None), P(PAIRS, None, None)),
        check_vma=False,
    )
```

```python
import jax
import jax.numpy as jnp
from jax import lax
from jax.experimental import pallas as pl
from jax.experimental.pallas import tpu as pltpu
from jax.sharding import Mesh
from jax.sharding import PartitionSpec as P

ITERS = 3
PAIRS = ("pairs_0", "pairs_1", "pairs_2")
PLANE = ("pairs_0", "pairs_1")
REP = 4
STEP = 8
LIMIT = 12 << 20
F32, BF16 = jnp.float32, jnp.bfloat16
NN = (((1,), (0,)), ((), ()))
NT = (((1,), (1,)), ((), ()))
TN = (((0,), (0,)), ((), ()))


def mm(a, b, dims):
    return lax.dot_general(a, b, dims, preferred_element_type=F32)


def shift(x, axis, count, by):
    return lax.ppermute(x, axis, [(i, (i + by) % count) for i in range(count)])


def swap(x, axis, count, bit):
    return lax.ppermute(x, axis, [(i, i ^ bit) for i in range(count)])


def store_shares(share_ref, n, rank_at, outs, at):
    for k, out in enumerate(outs):
        first = pl.multiple_of(lax.rem(rank_at + k, REP) * 32, 32)
        out[at] = share_ref[n, pl.ds(first, 32), :].astype(out.dtype)


def each_step(body_of):
    def one(step, carry):
        body_of(step)
        return carry

    lax.fori_loop(0, 32 // STEP, one, 0)


def integral_kernel(idx, *refs):
    pieces, (rot, o0, o1, o2, o3, occ, held, share) = refs[:8], refs[8:]
    for i, piece in enumerate(pieces):
        held[8 * i : 8 * i + 8] = piece[...]

    def some(step):
        halves = []
        for n in range(STEP):
            p = step * STEP + n
            left = mm(held[idx[1 + p], :128, :], rot[p, 0], NN)
            right = mm(held[idx[33 + p], :128, :], rot[p, 1], NN)
            left_hi, right_hi = left.astype(BF16), right.astype(BF16)
            left_lo = (left - left_hi.astype(F32)).astype(BF16)
            right_lo = (right - right_hi.astype(F32)).astype(BF16)
            halves.append((right_hi, right_lo, left_hi, left_lo))
        for n in range(STEP):
            right_hi, right_lo, left_hi, left_lo = halves[n]
            four = mm(
                jnp.concatenate([right_hi, right_lo], 1), jnp.concatenate([left_hi, left_lo], 1), TN
            )
            share[n] = four[:128, :128] + four[:128, 128:] + four[128:, :128]
        for n in range(STEP):
            p = step * STEP + n
            i, j = idx[1 + p], idx[33 + p]
            store_shares(share, n, idx[0], (o0, o1, o2, o3), p)
            occ[p] = held[i, 128:144, :].astype(F32)[:1] + held[j, 128:144, :].astype(F32)[:1]

    each_step(some)


def visible_rows(idx, p, first):
    rank = idx[1 + p]
    b = lax.broadcasted_iota(jnp.int32, (32, 128), 0) + first
    a = lax.broadcasted_iota(jnp.int32, (32, 128), 1)
    return (b < rank) & (a < rank)


def start_kernel(idx, own, r1, r2, r3, energy, occ, integral, denominator, amplitude):
    first = idx[0] * 32

    def one(p, carry):
        total = own[p] + r1[p].astype(F32) + r2[p].astype(F32) + r3[p].astype(F32)
        value = jnp.where(visible_rows(idx, p, first), total, 0.0)
        denom = energy[p] - occ[p]
        integral[p] = value
        denominator[p] = denom
        amplitude[p] = (-value / denom).astype(BF16)
        return carry

    lax.fori_loop(0, 32, one, 0, unroll=4)


def update_kernel(idx, own, r1, r2, r3, integral, denominator, amplitude):
    first = idx[0] * 32

    def one(p, carry):
        coupled = own[p] + r1[p].astype(F32) + r2[p].astype(F32) + r3[p].astype(F32)
        value = -(integral[p] - coupled) / denominator[p]
        amplitude[p] = jnp.where(visible_rows(idx, p, first), value, 0.0).astype(BF16)
        return carry

    lax.fori_loop(0, 32, one, 0, unroll=4)


def outgoing_kernel(idx, own, other, out):
    def one(d, carry):
        for s in range(2):
            out[d * 4 + s] = own[idx[d * 4 + s]]
            out[d * 4 + 2 + s] = other[idx[d * 4 + 2 + s]]
        return carry

    lax.fori_loop(0, 32, one, 0, unroll=4)


def columns_kernel(idx, margin, turned, out, rows):
    mine = pl.multiple_of(idx[0] * 32, 32)

    def some(step):
        for n in range(STEP):
            p = step * STEP + n
            for c in range(6):
                turned[p, c] = margin[p, c].T
                rows[n, 32 * c : 32 * c + 32, :] = turned[p, c, pl.ds(mine, 32), :]
            out[p] = rows[n].T

    each_step(some)


def relax_kernel(idx, weight, arrived, turned, columns, o0, o1, o2, o3, lefts, share):
    def some(step):
        for n in range(STEP):
            p = step * STEP + n
            for c in range(6):
                left = mm(arrived[idx[1 + p * 6 + c]], turned[p, c], NN)
                lefts[n, 32 * c : 32 * c + 32, :] = (left * weight[p * 6 + c]).astype(BF16)
        for n in range(STEP):
            share[n] = mm(columns[step * STEP + n], lefts[n], NN)
        for n in range(STEP):
            store_shares(share, n, idx[0], (o0, o1, o2, o3), step * STEP + n)

    each_step(some)


def density_kernel(idx, t0, t1, t2, t3, rot, amplitude, d0, d1, whole, sides, grams, acc):
    acc[...] = jnp.zeros_like(acc)
    mine = pl.multiple_of(idx[0] * 32, 32)

    def some(step):
        for n in range(STEP):
            for k, piece in enumerate((t0, t1, t2, t3)):
                first = pl.multiple_of(lax.rem(idx[0] + REP - k, REP) * 32, 32)
                whole[n, pl.ds(first, 32), :] = piece[step * STEP + n]
        for n in range(STEP):
            p = step * STEP + n
            amp_t = whole[n]
            amplitude[p] = amp_t.T
            sides[n, :128] = mm(rot[p, 0], amp_t, NT).astype(BF16)
            sides[n, 128:] = mm(rot[p, 1], amp_t, NN).astype(BF16)
        for n in range(STEP):
            rows = [sides[n, pl.ds(mine + at, 32), :] for at in (0, 128)]
            both = mm(jnp.concatenate(rows, 0), sides[n], NT)
            grams[2 * n] = both[:32, :128]
            grams[2 * n + 1] = both[32:, 128:]

        def add(k, carry):
            at = idx[1 + step * 2 * STEP + k]
            acc[at] = acc[at] + grams[k]
            return carry

        lax.fori_loop(0, 2 * STEP, add, 0)

    each_step(some)
    d0[...] = acc[:32]
    d1[...] = acc[32:]


def call(kernel, scalars, args, outs, scratch=(), cost=None):
    vmem, smem = pl.BlockSpec(memory_space=pltpu.VMEM), pl.BlockSpec(memory_space=pltpu.SMEM)
    return pl.pallas_call(
        kernel,
        in_specs=[smem] * len(scalars) + [vmem] * len(args),
        out_specs=[vmem] * len(outs),
        scratch_shapes=list(scratch),
        out_shape=outs,
        cost_estimate=cost,
        compiler_params=pltpu.CompilerParams(vmem_limit_bytes=LIMIT),
    )(*scalars, *args)


def struct(shape, dtype):
    return jax.ShapeDtypeStruct(shape, dtype)


def summed_over_rep(shares):
    return (shares[0],) + tuple(shift(shares[k], "rep", REP, k) for k in (1, 2, 3))


def body(
    factors,
    orbital_virtuals,
    occupied,
    pair_rotations,
    pair_energies,
    pair_orbitals,
    pair_ranks,
    margins,
    coupling_weight,
    send_slots,
    couplings,
):
    core, rep, col = lax.axis_index("pairs_2"), lax.axis_index("rep"), lax.axis_index("pairs_1")
    rep1 = rep[None].astype(jnp.int32)
    share3 = (32, 32, 128)
    share_structs = [struct(share3, F32)] + [struct(share3, BF16)] * 3
    share_scratch = pltpu.VMEM((STEP, 128, 128), F32)

    halves = mm(factors[0], orbital_virtuals[0], NN).astype(BF16)
    sent = jnp.concatenate([halves, jnp.broadcast_to(occupied[:, None], (16, 128))], 0)
    along_z = sent[None]
    for bit in (4, 2, 1):
        along_z = jnp.concatenate([along_z, swap(along_z, "pairs_0", 8, bit)], 0)
    pieces = [along_z] + [shift(along_z, "pairs_1", 4, k) for k in (1, 2, 3)]
    pieces += [shift(piece, "pairs_2", 2, 1) for piece in pieces]

    orb = pair_orbitals
    orb_z, orb_x, orb_c = orb // 8, (orb // 2) % 4, orb % 2
    apart = orb_z ^ lax.axis_index("pairs_0")
    z_at = (apart // 4) + (apart // 2) % 2 * 2 + apart % 2 * 4
    held_at = (((orb_c ^ core) * 4 + (col - orb_x) % 4) * 8 + z_at).T.reshape(-1)
    o0, o1, o2, o3, occ = call(
        integral_kernel,
        [jnp.concatenate([rep1, held_at])],
        [*pieces, pair_rotations],
        share_structs + [struct((32, 1, 128), F32)],
        [pltpu.VMEM((64, 144, 128), BF16), share_scratch],
    )

    turned, columns = call(
        columns_kernel,
        [rep1],
        [margins],
        [struct((32, 6, 128, 128), BF16), struct((32, 128, 192), BF16)],
        [pltpu.VMEM((STEP, 192, 128), BF16)],
        cost=pl.CostEstimate(
            flops=32 * 6 * 2 * 128 * 128 * 192, bytes_accessed=9 << 20, transcendentals=0
        ),
    )
    energy_col = lax.dynamic_slice_in_dim(pair_energies[:, 1], rep * 32, 32, 1)
    energy = energy_col[:, :, None] + pair_energies[:, 0][:, None, :]
    ranks = jnp.concatenate([rep1, pair_ranks])
    other_slots = shift(send_slots, "pairs_2", 2, 1)
    slots = jnp.concatenate(
        [lax.dynamic_index_in_dim(s.reshape(32, 2, 2), core, 1) for s in (send_slots, other_slots)],
        1,
    ).reshape(-1)
    owner = couplings // 2
    arrived_at = (owner // 2) * 4 + ((owner % 2) ^ core) * 2 + couplings % 2
    links = jnp.concatenate([rep1, arrived_at.reshape(-1)])
    weights = coupling_weight.reshape(-1)

    integral, denominator, amplitude = call(
        start_kernel,
        [ranks],
        [*summed_over_rep((o0, o1, o2, o3)), energy, occ],
        [struct(share3, F32), struct(share3, F32), struct(share3, BF16)],
    )
    for _ in range(ITERS):
        (outgoing,) = call(
            outgoing_kernel,
            [slots],
            [amplitude, shift(amplitude, "pairs_2", 2, 1)],
            [struct((128, 32, 128), BF16)],
        )
        arrived = lax.all_to_all(outgoing, PLANE, 0, 0, tiled=True)
        shares = call(
            relax_kernel,
            [links, weights],
            [arrived, turned, columns],
            share_structs,
            [pltpu.VMEM((STEP, 192, 128), BF16), share_scratch],
        )
        (amplitude,) = call(
            update_kernel,
            [ranks],
            [*summed_over_rep(shares), integral, denominator],
            [struct(share3, BF16)],
        )

    parts = [amplitude] + [shift(amplitude, "rep", REP, k) for k in (1, 2, 3)]
    dense_at = ((orb_c ^ core) * 32 + orb // 2).reshape(-1)
    final, d_own, d_other = call(
        density_kernel,
        [jnp.concatenate([rep1, dense_at])],
        [*parts, pair_rotations],
        [struct((32, 128, 128), BF16), struct(share3, F32), struct(share3, F32)],
        [
            pltpu.VMEM((STEP, 128, 128), BF16),
            pltpu.VMEM((STEP, 256, 128), BF16),
            pltpu.VMEM((2 * STEP, 32, 128), F32),
            pltpu.VMEM((64, 32, 128), F32),
        ],
    )
    both = (d_own + shift(d_other, "pairs_2", 2, 1)).astype(BF16)
    arrived = lax.all_to_all(both, PLANE, 0, 0, tiled=True)
    mine = jnp.sum(arrived.astype(F32), 0) / 128
    pair = jnp.stack([mine, swap(mine, "rep", REP, 1)])
    four = jnp.concatenate([pair, swap(pair, "rep", REP, 2)])
    order = rep ^ jnp.arange(REP, dtype=jnp.int32)
    chosen = order[:, None] == jnp.arange(REP, dtype=jnp.int32)[None]
    densities = sum(
        jnp.where(chosen[:, k, None, None], four[k][None], 0.0) for k in range(REP)
    ).reshape(1, 128, 128)
    return (final, densities)


def solution(mesh):
    finer = Mesh(
        mesh.devices.reshape(8, 4, 2, mesh.shape["rep"]), ("pairs_0", "pairs_1", "pairs_2", "rep")
    )
    return jax.shard_map(
        body,
        mesh=finer,
        in_specs=(
            P(PAIRS, "rep", None),
            P(PAIRS, None, None),
            P(PAIRS),
            P(PAIRS, None, None, None),
            P(PAIRS, None, None),
            P(PAIRS, None),
            P(PAIRS),
            P(PAIRS, None, None, None),
            P(PAIRS, None),
            P(PAIRS, None, None),
            P(PAIRS, None),
        ),
        out_specs=(P(PAIRS, None, None), P(PAIRS, None, None)),
        check_vma=False,
    )
```

```python
import jax
import jax.numpy as jnp
from jax import lax
from jax.experimental import pallas as pl
from jax.experimental.pallas import tpu as pltpu
from jax.sharding import Mesh
from jax.sharding import PartitionSpec as P

ITERS = 3
PAIRS = ("pairs_0", "pairs_1", "pairs_2")
PLANE = ("pairs_0", "pairs_1")
REP = 4
STEP = 8
LIMIT = 12 << 20
F32, BF16 = jnp.float32, jnp.bfloat16
NN = (((1,), (0,)), ((), ()))
NT = (((1,), (1,)), ((), ()))
TN = (((0,), (0,)), ((), ()))


def mm(a, b, dims):
    return lax.dot_general(a, b, dims, preferred_element_type=F32)


def shift(x, axis, count, by):
    return lax.ppermute(x, axis, [(i, (i + by) % count) for i in range(count)])


def swap(x, axis, count, bit):
    return lax.ppermute(x, axis, [(i, i ^ bit) for i in range(count)])


def store_shares(share_ref, n, rank_at, outs, at):
    for k, out in enumerate(outs):
        first = pl.multiple_of(lax.rem(rank_at + k, REP) * 32, 32)
        out[at] = share_ref[n, pl.ds(first, 32), :].astype(out.dtype)


def each_step(body_of):
    def one(step, carry):
        body_of(step)
        return carry

    lax.fori_loop(0, 32 // STEP, one, 0)


def integral_kernel(idx, *refs):
    pieces, (rot, o0, o1, o2, o3, occ, held, share) = refs[:8], refs[8:]
    for i, piece in enumerate(pieces):
        held[8 * i : 8 * i + 8] = piece[...]

    def some(step):
        halves = []
        for n in range(STEP):
            p = step * STEP + n
            left = mm(held[idx[1 + p], :128, :], rot[p, 0], NN)
            right = mm(held[idx[33 + p], :128, :], rot[p, 1], NN)
            left_hi, right_hi = left.astype(BF16), right.astype(BF16)
            left_lo = (left - left_hi.astype(F32)).astype(BF16)
            right_lo = (right - right_hi.astype(F32)).astype(BF16)
            halves.append((right_hi, right_lo, left_hi, left_lo))
        for n in range(STEP):
            right_hi, right_lo, left_hi, left_lo = halves[n]
            four = mm(
                jnp.concatenate([right_hi, right_lo], 1), jnp.concatenate([left_hi, left_lo], 1), TN
            )
            share[n] = four[:128, :128] + four[:128, 128:] + four[128:, :128]
        for n in range(STEP):
            p = step * STEP + n
            i, j = idx[1 + p], idx[33 + p]
            store_shares(share, n, idx[0], (o0, o1, o2, o3), p)
            occ[p] = held[i, 128:144, :].astype(F32)[:1] + held[j, 128:144, :].astype(F32)[:1]

    each_step(some)


def visible_rows(idx, p, first):
    rank = idx[1 + p]
    b = lax.broadcasted_iota(jnp.int32, (32, 128), 0) + first
    a = lax.broadcasted_iota(jnp.int32, (32, 128), 1)
    return (b < rank) & (a < rank)


def start_kernel(idx, own, r1, r2, r3, energy, occ, integral, denominator, amplitude):
    first = idx[0] * 32

    def one(p, carry):
        total = own[p] + r1[p].astype(F32) + r2[p].astype(F32) + r3[p].astype(F32)
        value = jnp.where(visible_rows(idx, p, first), total, 0.0)
        denom = energy[p] - occ[p]
        integral[p] = value
        denominator[p] = denom
        amplitude[p] = (-value / denom).astype(BF16)
        return carry

    lax.fori_loop(0, 32, one, 0, unroll=4)


def update_kernel(idx, own, r1, r2, r3, integral, denominator, amplitude):
    first = idx[0] * 32

    def one(p, carry):
        coupled = own[p] + r1[p].astype(F32) + r2[p].astype(F32) + r3[p].astype(F32)
        value = -(integral[p] - coupled) / denominator[p]
        amplitude[p] = jnp.where(visible_rows(idx, p, first), value, 0.0).astype(BF16)
        return carry

    lax.fori_loop(0, 32, one, 0, unroll=4)


def outgoing_kernel(idx, own, other, out):
    def one(d, carry):
        for s in range(2):
            out[d * 4 + s] = own[idx[d * 4 + s]]
            out[d * 4 + 2 + s] = other[idx[d * 4 + 2 + s]]
        return carry

    lax.fori_loop(0, 32, one, 0, unroll=4)


def columns_kernel(idx, margin, turned, out, rows):
    mine = pl.multiple_of(idx[0] * 32, 32)

    def some(step):
        for n in range(STEP):
            p = step * STEP + n
            for c in range(6):
                turned[p, c] = margin[p, c].T
                rows[n, 32 * c : 32 * c + 32, :] = turned[p, c, pl.ds(mine, 32), :]
            out[p] = rows[n].T

    each_step(some)


def relax_kernel(idx, weight, arrived, turned, columns, o0, o1, o2, o3, lefts, share):
    def some(step):
        for n in range(STEP):
            p = step * STEP + n
            for c in range(6):
                left = mm(arrived[idx[1 + p * 6 + c]], turned[p, c], NN)
                lefts[n, 32 * c : 32 * c + 32, :] = (left * weight[p * 6 + c]).astype(BF16)
        for n in range(STEP):
            share[n] = mm(columns[step * STEP + n], lefts[n], NN)
        for n in range(STEP):
            store_shares(share, n, idx[0], (o0, o1, o2, o3), step * STEP + n)

    each_step(some)


def density_kernel(idx, t0, t1, t2, t3, rot, amplitude, d0, d1, whole, sides, grams, acc):
    acc[...] = jnp.zeros_like(acc)
    mine = pl.multiple_of(idx[0] * 32, 32)

    def some(step):
        for n in range(STEP):
            for k, piece in enumerate((t0, t1, t2, t3)):
                first = pl.multiple_of(lax.rem(idx[0] + REP - k, REP) * 32, 32)
                whole[n, pl.ds(first, 32), :] = piece[step * STEP + n]
        for n in range(STEP):
            p = step * STEP + n
            amp_t = whole[n]
            amplitude[p] = amp_t.T
            sides[n, :128] = mm(rot[p, 0], amp_t, NT).astype(BF16)
            sides[n, 128:] = mm(rot[p, 1], amp_t, NN).astype(BF16)
        for n in range(STEP):
            rows = [sides[n, pl.ds(mine + at, 32), :] for at in (0, 128)]
            both = mm(jnp.concatenate(rows, 0), sides[n], NT)
            grams[2 * n] = both[:32, :128]
            grams[2 * n + 1] = both[32:, 128:]

        def add(k, carry):
            at = idx[1 + step * 2 * STEP + k]
            acc[at] = acc[at] + grams[k]
            return carry

        lax.fori_loop(0, 2 * STEP, add, 0)

    each_step(some)
    d0[...] = acc[:32]
    d1[...] = acc[32:]


def call(kernel, scalars, args, outs, scratch=(), cost=None):
    vmem, smem = pl.BlockSpec(memory_space=pltpu.VMEM), pl.BlockSpec(memory_space=pltpu.SMEM)
    return pl.pallas_call(
        kernel,
        in_specs=[smem] * len(scalars) + [vmem] * len(args),
        out_specs=[vmem] * len(outs),
        scratch_shapes=list(scratch),
        out_shape=outs,
        cost_estimate=cost,
        compiler_params=pltpu.CompilerParams(vmem_limit_bytes=LIMIT),
    )(*scalars, *args)


def struct(shape, dtype):
    return jax.ShapeDtypeStruct(shape, dtype)


def summed_over_rep(shares):
    return (shares[0],) + tuple(shift(shares[k], "rep", REP, k) for k in (1, 2, 3))


def body(
    factors,
    orbital_virtuals,
    occupied,
    pair_rotations,
    pair_energies,
    pair_orbitals,
    pair_ranks,
    margins,
    coupling_weight,
    send_slots,
    couplings,
):
    core, rep, col = lax.axis_index("pairs_2"), lax.axis_index("rep"), lax.axis_index("pairs_1")
    rep1 = rep[None].astype(jnp.int32)
    share3 = (32, 32, 128)
    share_structs = [struct(share3, F32)] + [struct(share3, BF16)] * 3
    share_scratch = pltpu.VMEM((STEP, 128, 128), F32)

    halves = mm(factors[0], orbital_virtuals[0], NN).astype(BF16)
    sent = jnp.concatenate([halves, jnp.broadcast_to(occupied[:, None], (16, 128))], 0)
    along_z = sent[None]
    for bit in (4, 2, 1):
        along_z = jnp.concatenate([along_z, swap(along_z, "pairs_0", 8, bit)], 0)
    pieces = [along_z] + [shift(along_z, "pairs_1", 4, k) for k in (1, 2, 3)]
    pieces += [shift(piece, "pairs_2", 2, 1) for piece in pieces]

    orb = pair_orbitals
    orb_z, orb_x, orb_c = orb // 8, (orb // 2) % 4, orb % 2
    apart = orb_z ^ lax.axis_index("pairs_0")
    z_at = (apart // 4) + (apart // 2) % 2 * 2 + apart % 2 * 4
    held_at = (((orb_c ^ core) * 4 + (col - orb_x) % 4) * 8 + z_at).T.reshape(-1)
    o0, o1, o2, o3, occ = call(
        integral_kernel,
        [jnp.concatenate([rep1, held_at])],
        [*pieces, pair_rotations],
        share_structs + [struct((32, 1, 128), F32)],
        [pltpu.VMEM((64, 144, 128), BF16), share_scratch],
    )

    energy_col = lax.dynamic_slice_in_dim(pair_energies[:, 1], rep * 32, 32, 1)
    energy = energy_col[:, :, None] + pair_energies[:, 0][:, None, :]
    ranks = jnp.concatenate([rep1, pair_ranks])
    other_slots = shift(send_slots, "pairs_2", 2, 1)
    slots = jnp.concatenate(
        [lax.dynamic_index_in_dim(s.reshape(32, 2, 2), core, 1) for s in (send_slots, other_slots)],
        1,
    ).reshape(-1)
    owner = couplings // 2
    arrived_at = (owner // 2) * 4 + ((owner % 2) ^ core) * 2 + couplings % 2
    links = jnp.concatenate([rep1, arrived_at.reshape(-1)])
    weights = coupling_weight.reshape(-1)

    integral, denominator, amplitude = call(
        start_kernel,
        [ranks],
        [*summed_over_rep((o0, o1, o2, o3)), energy, occ],
        [struct(share3, F32), struct(share3, F32), struct(share3, BF16)],
    )
    amplitude, rep_late = lax.optimization_barrier((amplitude, rep1))
    turned, columns = call(
        columns_kernel,
        [rep_late],
        [margins],
        [struct((32, 6, 128, 128), BF16), struct((32, 128, 192), BF16)],
        [pltpu.VMEM((STEP, 192, 128), BF16)],
        cost=pl.CostEstimate(
            flops=32 * 6 * 2 * 128 * 128 * 192, bytes_accessed=9 << 20, transcendentals=0
        ),
    )
    for turn in range(ITERS):
        (outgoing,) = call(
            outgoing_kernel,
            [slots],
            [amplitude, shift(amplitude, "pairs_2", 2, 1)],
            [struct((128, 32, 128), BF16)],
        )
        if turn == 0:
            outgoing, links, weights, turned, columns, ranks = lax.optimization_barrier(
                (outgoing, links, weights, turned, columns, ranks)
            )
        arrived = lax.all_to_all(outgoing, PLANE, 0, 0, tiled=True)
        shares = call(
            relax_kernel,
            [links, weights],
            [arrived, turned, columns],
            share_structs,
            [pltpu.VMEM((STEP, 192, 128), BF16), share_scratch],
        )
        (amplitude,) = call(
            update_kernel,
            [ranks],
            [*summed_over_rep(shares), integral, denominator],
            [struct(share3, BF16)],
        )

    parts = [amplitude] + [shift(amplitude, "rep", REP, k) for k in (1, 2, 3)]
    dense_at = ((orb_c ^ core) * 32 + orb // 2).reshape(-1)
    final, d_own, d_other = call(
        density_kernel,
        [jnp.concatenate([rep1, dense_at])],
        [*parts, pair_rotations],
        [struct((32, 128, 128), BF16), struct(share3, F32), struct(share3, F32)],
        [
            pltpu.VMEM((STEP, 128, 128), BF16),
            pltpu.VMEM((STEP, 256, 128), BF16),
            pltpu.VMEM((2 * STEP, 32, 128), F32),
            pltpu.VMEM((64, 32, 128), F32),
        ],
    )
    order = rep ^ jnp.arange(REP, dtype=jnp.int32)
    chosen = order[:, None] == jnp.arange(REP, dtype=jnp.int32)[None]
    chosen = jnp.broadcast_to(chosen.astype(F32)[:, :, None, None], (REP, REP, 1, 128))
    both = (d_own + shift(d_other, "pairs_2", 2, 1)).astype(BF16)
    both, chosen, final = lax.optimization_barrier((both, chosen, final))
    arrived = lax.all_to_all(both, PLANE, 0, 0, tiled=True)
    mine = jnp.sum(arrived.astype(F32), 0) / 128
    pair = jnp.stack([mine, swap(mine, "rep", REP, 1)])
    four = jnp.concatenate([pair, swap(pair, "rep", REP, 2)])
    densities = sum(
        chosen[:, k] * four[k][None] for k in range(REP)
    ).reshape(1, 128, 128)
    return (final, densities)


def solution(mesh):
    finer = Mesh(
        mesh.devices.reshape(8, 4, 2, mesh.shape["rep"]), ("pairs_0", "pairs_1", "pairs_2", "rep")
    )
    return jax.shard_map(
        body,
        mesh=finer,
        in_specs=(
            P(PAIRS, "rep", None),
            P(PAIRS, None, None),
            P(PAIRS),
            P(PAIRS, None, None, None),
            P(PAIRS, None, None),
            P(PAIRS, None),
            P(PAIRS),
            P(PAIRS, None, None, None),
            P(PAIRS, None),
            P(PAIRS, None, None),
            P(PAIRS, None),
        ),
        out_specs=(P(PAIRS, None, None), P(PAIRS, None, None)),
        check_vma=False,
    )
```

```python
import jax
import jax.numpy as jnp
from jax import lax
from jax.experimental import pallas as pl
from jax.experimental.pallas import tpu as pltpu
from jax.sharding import Mesh
from jax.sharding import PartitionSpec as P

ITERS = 3
PAIRS = ("pairs_0", "pairs_1", "pairs_2")
PLANE = ("pairs_0", "pairs_1")
REP = 4
STEP = 8
LIMIT = 12 << 20
F32, BF16 = jnp.float32, jnp.bfloat16
NN = (((1,), (0,)), ((), ()))
NT = (((1,), (1,)), ((), ()))
TN = (((0,), (0,)), ((), ()))


def mm(a, b, dims):
    return lax.dot_general(a, b, dims, preferred_element_type=F32)


def shift(x, axis, count, by):
    return lax.ppermute(x, axis, [(i, (i + by) % count) for i in range(count)])


def swap(x, axis, count, bit):
    return lax.ppermute(x, axis, [(i, i ^ bit) for i in range(count)])


def store_shares(share_ref, n, rank_at, outs, at):
    for k, out in enumerate(outs):
        first = pl.multiple_of(lax.rem(rank_at + k, REP) * 32, 32)
        out[at] = share_ref[n, pl.ds(first, 32), :].astype(out.dtype)


def each_step(body_of):
    def one(step, carry):
        body_of(step)
        return carry

    lax.fori_loop(0, 32 // STEP, one, 0)


def integral_kernel(idx, *refs):
    pieces, (rot, o0, o1, o2, o3, occ, held, share) = refs[:16], refs[16:]
    step = pl.program_id(0)

    @pl.when(step == 0)
    def _():
        for i, piece in enumerate(pieces):
            first = i % 8 * 8 + i // 8 * 4
            held[first : first + 4] = piece[...]

    halves = []
    for n in range(STEP):
        p = step * STEP + n
        left = mm(held[idx[1 + p], :128, :], rot[n, 0], NN)
        right = mm(held[idx[33 + p], :128, :], rot[n, 1], NN)
        left_hi, right_hi = left.astype(BF16), right.astype(BF16)
        left_lo = (left - left_hi.astype(F32)).astype(BF16)
        right_lo = (right - right_hi.astype(F32)).astype(BF16)
        halves.append((right_hi, right_lo, left_hi, left_lo))
    for n in range(STEP):
        right_hi, right_lo, left_hi, left_lo = halves[n]
        four = mm(
            jnp.concatenate([right_hi, right_lo], 1), jnp.concatenate([left_hi, left_lo], 1), TN
        )
        share[n] = four[:128, :128] + four[:128, 128:] + four[128:, :128]
    for n in range(STEP):
        p = step * STEP + n
        i, j = idx[1 + p], idx[33 + p]
        store_shares(share, n, idx[0], (o0, o1, o2, o3), p)
        occ[p] = held[i, 128:144, :].astype(F32)[:1] + held[j, 128:144, :].astype(F32)[:1]


def visible_rows(idx, p, first):
    rank = idx[1 + p]
    b = lax.broadcasted_iota(jnp.int32, (32, 128), 0) + first
    a = lax.broadcasted_iota(jnp.int32, (32, 128), 1)
    return (b < rank) & (a < rank)


def start_kernel(idx, own, r1, r2, r3, energy, occ, integral, denominator, amplitude):
    first = idx[0] * 32

    def one(p, carry):
        total = own[p] + r1[p].astype(F32) + r2[p].astype(F32) + r3[p].astype(F32)
        value = jnp.where(visible_rows(idx, p, first), total, 0.0)
        denom = energy[p] - occ[p]
        integral[p] = value
        denominator[p] = denom
        amplitude[p] = (-value / denom).astype(BF16)
        return carry

    lax.fori_loop(0, 32, one, 0, unroll=4)


def update_kernel(idx, own, r1, r2, r3, integral, denominator, amplitude):
    first = idx[0] * 32

    def one(p, carry):
        coupled = own[p] + r1[p].astype(F32) + r2[p].astype(F32) + r3[p].astype(F32)
        value = -(integral[p] - coupled) / denominator[p]
        amplitude[p] = jnp.where(visible_rows(idx, p, first), value, 0.0).astype(BF16)
        return carry

    lax.fori_loop(0, 32, one, 0, unroll=4)


def outgoing_kernel(idx, own, other, out):
    def one(d, carry):
        for s in range(2):
            out[d * 4 + s] = own[idx[d * 4 + s]]
            out[d * 4 + 2 + s] = other[idx[d * 4 + 2 + s]]
        return carry

    lax.fori_loop(0, 32, one, 0, unroll=4)


def columns_kernel(idx, margin, turned, out, rows):
    step, mine = pl.program_id(0), pl.multiple_of(idx[0] * 32, 32)
    for n in range(STEP):
        for c in range(6):
            turned[step * STEP + n, c] = margin[n, c].T
    for n in range(STEP):
        for c in range(6):
            rows[n, 32 * c : 32 * c + 32, :] = turned[step * STEP + n, c, pl.ds(mine, 32), :]
    for n in range(STEP):
        out[step * STEP + n] = rows[n].T


def relax_kernel(idx, weight, arrived, turned, columns, o0, o1, o2, o3, lefts, share):
    def some(step):
        for n in range(STEP):
            p = step * STEP + n
            for c in range(6):
                left = mm(arrived[idx[1 + p * 6 + c]], turned[p, c], NN)
                lefts[n, 32 * c : 32 * c + 32, :] = (left * weight[p * 6 + c]).astype(BF16)
        for n in range(STEP):
            share[n] = mm(columns[step * STEP + n], lefts[n], NN)
        for n in range(STEP):
            store_shares(share, n, idx[0], (o0, o1, o2, o3), step * STEP + n)

    each_step(some)


def density_kernel(idx, t0, t1, t2, t3, rot, amplitude, d0, d1, whole, sides, grams, acc):
    step, mine = pl.program_id(0), pl.multiple_of(idx[0] * 32, 32)

    @pl.when(step == 0)
    def _():
        acc[...] = jnp.zeros_like(acc)

    for n in range(STEP):
        for k, piece in enumerate((t0, t1, t2, t3)):
            first = pl.multiple_of(lax.rem(idx[0] + REP - k, REP) * 32, 32)
            whole[n, pl.ds(first, 32), :] = piece[step * STEP + n]
    for n in range(STEP):
        p = step * STEP + n
        amp_t = whole[n]
        amplitude[p] = amp_t.T
        sides[n, :128] = mm(rot[n, 0], amp_t, NT).astype(BF16)
        sides[n, 128:] = mm(rot[n, 1], amp_t, NN).astype(BF16)
    for n in range(STEP):
        rows = [sides[n, pl.ds(mine + at, 32), :] for at in (0, 128)]
        both = mm(jnp.concatenate(rows, 0), sides[n], NT)
        grams[2 * n] = both[:32, :128]
        grams[2 * n + 1] = both[32:, 128:]

    def add(k, carry):
        at = idx[1 + step * 2 * STEP + k]
        acc[at] = acc[at] + grams[k]
        return carry

    lax.fori_loop(0, 2 * STEP, add, 0)

    @pl.when(step == pl.num_programs(0) - 1)
    def _():
        d0[...] = acc[:32]
        d1[...] = acc[32:]


def call(kernel, scalars, args, outs, scratch=(), cost=None, streamed=None, limit=LIMIT):
    vmem, smem = pl.BlockSpec(memory_space=pltpu.VMEM), pl.BlockSpec(memory_space=pltpu.SMEM)
    specs, grid = [smem] * len(scalars) + [vmem] * len(args), ()
    if streamed is not None:
        block = (STEP, *streamed.shape[1:])
        specs.append(pl.BlockSpec(block, lambda g: (g,) + (0,) * (len(block) - 1)))
        args, grid = [*args, streamed], (32 // STEP,)
    return pl.pallas_call(
        kernel,
        grid=grid,
        in_specs=specs,
        out_specs=[vmem] * len(outs),
        scratch_shapes=list(scratch),
        out_shape=outs,
        cost_estimate=cost,
        compiler_params=pltpu.CompilerParams(vmem_limit_bytes=limit),
    )(*scalars, *args)


def struct(shape, dtype):
    return jax.ShapeDtypeStruct(shape, dtype)


def exchanged_over_rep(shares):
    far = {k: shift(shares[k], "rep", REP, k) for k in (2, 1, 3)}
    return shares[0], far[1], far[2], far[3]


def body(
    factors,
    orbital_virtuals,
    occupied,
    pair_rotations,
    pair_energies,
    pair_orbitals,
    pair_ranks,
    margins,
    coupling_weight,
    send_slots,
    couplings,
):
    core, rep, col = lax.axis_index("pairs_2"), lax.axis_index("rep"), lax.axis_index("pairs_1")
    rep1 = rep[None].astype(jnp.int32)
    share3 = (32, 32, 128)
    share_structs = [struct(share3, F32)] + [struct(share3, BF16)] * 3
    share_scratch = pltpu.VMEM((STEP, 128, 128), F32)

    halves = mm(factors[0], orbital_virtuals[0], NN).astype(BF16)
    sent = jnp.concatenate([halves, jnp.broadcast_to(occupied[:, None], (16, 128))], 0)
    near = sent[None]
    for bit in (4, 2):
        near = jnp.concatenate([near, swap(near, "pairs_0", 8, bit)], 0)
    pieces = []
    for group in (near, swap(near, "pairs_0", 8, 1)):
        along_x = [group] + [shift(group, "pairs_1", 4, k) for k in (1, 2, 3)]
        pieces += along_x + [shift(piece, "pairs_2", 2, 1) for piece in along_x]

    orb = pair_orbitals
    orb_z, orb_x, orb_c = orb // 8, (orb // 2) % 4, orb % 2
    apart = orb_z ^ lax.axis_index("pairs_0")
    z_at = (apart // 4) + (apart // 2) % 2 * 2 + apart % 2 * 4
    held_at = (((orb_c ^ core) * 4 + (col - orb_x) % 4) * 8 + z_at).T.reshape(-1)
    o0, o1, o2, o3, occ = call(
        integral_kernel,
        [jnp.concatenate([rep1, held_at])],
        pieces,
        share_structs + [struct((32, 1, 128), F32)],
        [pltpu.VMEM((64, 144, 128), BF16), share_scratch],
        streamed=pair_rotations,
        limit=12 << 20,
    )

    energy_col = lax.dynamic_slice_in_dim(pair_energies[:, 1], rep * 32, 32, 1)
    energy = energy_col[:, :, None] + pair_energies[:, 0][:, None, :]
    ranks = jnp.concatenate([rep1, pair_ranks])
    other_slots = shift(send_slots, "pairs_2", 2, 1)
    slots = jnp.concatenate(
        [lax.dynamic_index_in_dim(s.reshape(32, 2, 2), core, 1) for s in (send_slots, other_slots)],
        1,
    ).reshape(-1)
    owner = couplings // 2
    arrived_at = (owner // 2) * 4 + ((owner % 2) ^ core) * 2 + couplings % 2
    links = jnp.concatenate([rep1, arrived_at.reshape(-1)])
    weights = coupling_weight.reshape(-1)

    integral, denominator, amplitude = call(
        start_kernel,
        [ranks],
        [*exchanged_over_rep((o0, o1, o2, o3)), energy, occ],
        [struct(share3, F32), struct(share3, F32), struct(share3, BF16)],
    )
    amplitude, rep_late = lax.optimization_barrier((amplitude, rep1))
    turned, columns = call(
        columns_kernel,
        [rep_late],
        [],
        [struct((32, 6, 128, 128), BF16), struct((32, 128, 192), BF16)],
        [pltpu.VMEM((STEP, 192, 128), BF16)],
        streamed=margins,
        limit=42 << 20,
        cost=pl.CostEstimate(
            flops=32 * 6 * 2 * 128 * 128 * 192, bytes_accessed=9 << 20, transcendentals=0
        ),
    )
    for turn in range(ITERS):
        (outgoing,) = call(
            outgoing_kernel,
            [slots],
            [amplitude, shift(amplitude, "pairs_2", 2, 1)],
            [struct((128, 32, 128), BF16)],
        )
        if turn == 0:
            outgoing, links, weights, turned, columns, ranks = lax.optimization_barrier(
                (outgoing, links, weights, turned, columns, ranks)
            )
        arrived = lax.all_to_all(outgoing, PLANE, 0, 0, tiled=True)
        shares = call(
            relax_kernel,
            [links, weights],
            [arrived, turned, columns],
            share_structs,
            [pltpu.VMEM((STEP, 192, 128), BF16), share_scratch],
        )
        (amplitude,) = call(
            update_kernel,
            [ranks],
            [*exchanged_over_rep(shares), integral, denominator],
            [struct(share3, BF16)],
        )

    parts = exchanged_over_rep([amplitude] * REP)
    dense_at = ((orb_c ^ core) * 32 + orb // 2).reshape(-1)
    final, d_own, d_other = call(
        density_kernel,
        [jnp.concatenate([rep1, dense_at])],
        parts,
        [struct((32, 128, 128), BF16), struct(share3, F32), struct(share3, F32)],
        [
            pltpu.VMEM((STEP, 128, 128), BF16),
            pltpu.VMEM((STEP, 256, 128), BF16),
            pltpu.VMEM((2 * STEP, 32, 128), F32),
            pltpu.VMEM((64, 32, 128), F32),
        ],
        streamed=pair_rotations,
        limit=12 << 20,
    )
    order = rep ^ jnp.arange(REP, dtype=jnp.int32)
    chosen = order[:, None] == jnp.arange(REP, dtype=jnp.int32)[None]
    chosen = jnp.broadcast_to(chosen.astype(F32)[:, :, None, None], (REP, REP, 1, 128))
    both = (d_own + shift(d_other, "pairs_2", 2, 1)).astype(BF16)
    both, chosen, final = lax.optimization_barrier((both, chosen, final))
    arrived = lax.all_to_all(both, PLANE, 0, 0, tiled=True)
    mine = jnp.sum(arrived.astype(F32), 0) / 128
    pair = jnp.stack([mine, swap(mine, "rep", REP, 1)])
    four = jnp.concatenate([pair, swap(pair, "rep", REP, 2)])
    densities = sum(
        chosen[:, k] * four[k][None] for k in range(REP)
    ).reshape(1, 128, 128)
    return (final, densities)


def solution(mesh):
    finer = Mesh(
        mesh.devices.reshape(8, 4, 2, mesh.shape["rep"]), ("pairs_0", "pairs_1", "pairs_2", "rep")
    )
    return jax.shard_map(
        body,
        mesh=finer,
        in_specs=(
            P(PAIRS, "rep", None),
            P(PAIRS, None, None),
            P(PAIRS),
            P(PAIRS, None, None, None),
            P(PAIRS, None, None),
            P(PAIRS, None),
            P(PAIRS),
            P(PAIRS, None, None, None),
            P(PAIRS, None),
            P(PAIRS, None, None),
            P(PAIRS, None),
        ),
        out_specs=(P(PAIRS, None, None), P(PAIRS, None, None)),
        check_vma=False,
    )
```

```python
import jax
import jax.numpy as jnp
from jax import lax
from jax.experimental import pallas as pl
from jax.experimental.pallas import tpu as pltpu
from jax.sharding import Mesh
from jax.sharding import PartitionSpec as P

ITERS = 3
PAIRS = ("pairs_0", "pairs_1", "pairs_2")
PLANE = ("pairs_0", "pairs_1")
REP = 4
STEP = 8
LIMIT = 12 << 20
F32, BF16 = jnp.float32, jnp.bfloat16
NN = (((1,), (0,)), ((), ()))
NT = (((1,), (1,)), ((), ()))
TN = (((0,), (0,)), ((), ()))


def mm(a, b, dims):
    return lax.dot_general(a, b, dims, preferred_element_type=F32)


def shift(x, axis, count, by):
    return lax.ppermute(x, axis, [(i, (i + by) % count) for i in range(count)])


def swap(x, axis, count, bit):
    return lax.ppermute(x, axis, [(i, i ^ bit) for i in range(count)])


def store_shares(share_ref, n, rank_at, outs, at):
    for k, out in enumerate(outs):
        first = pl.multiple_of(lax.rem(rank_at + k, REP) * 32, 32)
        out[at] = share_ref[n, pl.ds(first, 32), :].astype(out.dtype)


def each_step(body_of):
    def one(step, carry):
        body_of(step)
        return carry

    lax.fori_loop(0, 32 // STEP, one, 0)


def integral_kernel(idx, *refs):
    pieces, (rot, o0, o1, o2, o3, occ, held, share) = refs[:16], refs[16:]
    step = pl.program_id(0)

    @pl.when(step == 0)
    def _():
        for i, piece in enumerate(pieces):
            first = i % 8 * 8 + i // 8 * 4
            held[first : first + 4] = piece[...]

    halves = []
    for n in range(STEP):
        p = step * STEP + n
        left = mm(held[idx[1 + p], :128, :], rot[n, 0], NN)
        right = mm(held[idx[33 + p], :128, :], rot[n, 1], NN)
        left_hi, right_hi = left.astype(BF16), right.astype(BF16)
        left_lo = (left - left_hi.astype(F32)).astype(BF16)
        right_lo = (right - right_hi.astype(F32)).astype(BF16)
        halves.append((right_hi, right_lo, left_hi, left_lo))
    for n in range(STEP):
        right_hi, right_lo, left_hi, left_lo = halves[n]
        four = mm(
            jnp.concatenate([right_hi, right_lo], 1), jnp.concatenate([left_hi, left_lo], 1), TN
        )
        share[n] = four[:128, :128] + four[:128, 128:] + four[128:, :128]
    for n in range(STEP):
        p = step * STEP + n
        i, j = idx[1 + p], idx[33 + p]
        store_shares(share, n, idx[0], (o0, o1, o2, o3), p)
        occ[p] = held[i, 128:144, :].astype(F32)[:1] + held[j, 128:144, :].astype(F32)[:1]


def visible_rows(idx, p, first):
    rank = idx[1 + p]
    b = lax.broadcasted_iota(jnp.int32, (32, 128), 0) + first
    a = lax.broadcasted_iota(jnp.int32, (32, 128), 1)
    return (b < rank) & (a < rank)


def start_kernel(idx, own, r1, r2, r3, energy, occ, integral, denominator, amplitude):
    first = idx[0] * 32

    def one(p, carry):
        total = own[p] + r1[p].astype(F32) + r2[p].astype(F32) + r3[p].astype(F32)
        value = jnp.where(visible_rows(idx, p, first), total, 0.0)
        denom = energy[p] - occ[p]
        integral[p] = value
        denominator[p] = denom
        amplitude[p] = (-value / denom).astype(BF16)
        return carry

    lax.fori_loop(0, 32, one, 0, unroll=4)


def update_kernel(idx, own, r1, r2, r3, integral, denominator, amplitude):
    first = idx[0] * 32

    def one(p, carry):
        coupled = own[p] + r1[p].astype(F32) + r2[p].astype(F32) + r3[p].astype(F32)
        value = -(integral[p] - coupled) / denominator[p]
        amplitude[p] = jnp.where(visible_rows(idx, p, first), value, 0.0).astype(BF16)
        return carry

    lax.fori_loop(0, 32, one, 0, unroll=4)


def outgoing_kernel(idx, own, other, out):
    def one(d, carry):
        for s in range(2):
            out[d * 4 + s] = own[idx[d * 4 + s]]
            out[d * 4 + 2 + s] = other[idx[d * 4 + 2 + s]]
        return carry

    lax.fori_loop(0, 32, one, 0, unroll=4)


def columns_kernel(idx, margin, turned, out, rows):
    step, mine = pl.program_id(0), pl.multiple_of(idx[0] * 32, 32)
    for n in range(STEP):
        for c in range(6):
            turned[step * STEP + n, c] = margin[n, c].T
    for n in range(STEP):
        for c in range(6):
            rows[n, 32 * c : 32 * c + 32, :] = turned[step * STEP + n, c, pl.ds(mine, 32), :]
    for n in range(STEP):
        out[step * STEP + n] = rows[n].T


def relax_kernel(idx, weight, arrived, turned, columns, o0, o1, o2, o3, lefts, share):
    def some(step):
        for n in range(STEP):
            p = step * STEP + n
            for c in range(6):
                left = mm(arrived[idx[1 + p * 6 + c]], turned[p, c], NN)
                lefts[n, 32 * c : 32 * c + 32, :] = (left * weight[p * 6 + c]).astype(BF16)
        for n in range(STEP):
            share[n] = mm(columns[step * STEP + n], lefts[n], NN)
        for n in range(STEP):
            store_shares(share, n, idx[0], (o0, o1, o2, o3), step * STEP + n)

    each_step(some)


def density_kernel(idx, t0, t1, t2, t3, rot, amplitude, d0, d1, whole, sides, grams, acc):
    step, mine = pl.program_id(0), pl.multiple_of(idx[0] * 32, 32)

    @pl.when(step == 0)
    def _():
        acc[...] = jnp.zeros_like(acc)

    for n in range(STEP):
        for k, piece in enumerate((t0, t1, t2, t3)):
            first = pl.multiple_of(lax.rem(idx[0] + REP - k, REP) * 32, 32)
            whole[n, pl.ds(first, 32), :] = piece[step * STEP + n]
    for n in range(STEP):
        p = step * STEP + n
        amp_t = whole[n]
        amplitude[p] = amp_t.T
        sides[n, :128] = mm(rot[n, 0], amp_t, NT).astype(BF16)
        sides[n, 128:] = mm(rot[n, 1], amp_t, NN).astype(BF16)
    for n in range(STEP):
        rows = [sides[n, pl.ds(mine + at, 32), :] for at in (0, 128)]
        both = mm(jnp.concatenate(rows, 0), sides[n], NT)
        grams[2 * n] = both[:32, :128]
        grams[2 * n + 1] = both[32:, 128:]

    def add(k, carry):
        at = idx[1 + step * 2 * STEP + k]
        acc[at] = acc[at] + grams[k]
        return carry

    lax.fori_loop(0, 2 * STEP, add, 0)

    @pl.when(step == pl.num_programs(0) - 1)
    def _():
        d0[...] = acc[:32]
        d1[...] = acc[32:]


def call(kernel, scalars, args, outs, scratch=(), cost=None, streamed=None, limit=LIMIT):
    vmem, smem = pl.BlockSpec(memory_space=pltpu.VMEM), pl.BlockSpec(memory_space=pltpu.SMEM)
    specs, grid = [smem] * len(scalars) + [vmem] * len(args), ()
    if streamed is not None:
        block = (STEP, *streamed.shape[1:])
        specs.append(pl.BlockSpec(block, lambda g: (g,) + (0,) * (len(block) - 1)))
        args, grid = [*args, streamed], (32 // STEP,)
    return pl.pallas_call(
        kernel,
        grid=grid,
        in_specs=specs,
        out_specs=[vmem] * len(outs),
        scratch_shapes=list(scratch),
        out_shape=outs,
        cost_estimate=cost,
        compiler_params=pltpu.CompilerParams(vmem_limit_bytes=limit),
    )(*scalars, *args)


def struct(shape, dtype):
    return jax.ShapeDtypeStruct(shape, dtype)


def exchanged_over_rep(shares):
    far = {k: shift(shares[k], "rep", REP, k) for k in (2, 1, 3)}
    return shares[0], far[1], far[2], far[3]


def body(
    factors,
    orbital_virtuals,
    occupied,
    pair_rotations,
    pair_energies,
    pair_orbitals,
    pair_ranks,
    margins,
    coupling_weight,
    send_slots,
    couplings,
):
    core, rep, col = lax.axis_index("pairs_2"), lax.axis_index("rep"), lax.axis_index("pairs_1")
    rep1 = rep[None].astype(jnp.int32)
    share3 = (32, 32, 128)
    share_structs = [struct(share3, F32)] + [struct(share3, BF16)] * 3
    share_scratch = pltpu.VMEM((STEP, 128, 128), F32)

    halves = mm(factors[0], orbital_virtuals[0], NN).astype(BF16)
    sent = jnp.concatenate([halves, jnp.broadcast_to(occupied[:, None], (16, 128))], 0)
    near = sent[None]
    for bit in (4, 2):
        near = jnp.concatenate([near, swap(near, "pairs_0", 8, bit)], 0)
    pieces = []
    for group in (near, swap(near, "pairs_0", 8, 1)):
        along_x = [group] + [shift(group, "pairs_1", 4, k) for k in (1, 2, 3)]
        pieces += along_x + [shift(piece, "pairs_2", 2, 1) for piece in along_x]

    orb = pair_orbitals
    orb_z, orb_x, orb_c = orb // 8, (orb // 2) % 4, orb % 2
    apart = orb_z ^ lax.axis_index("pairs_0")
    z_at = (apart // 4) + (apart // 2) % 2 * 2 + apart % 2 * 4
    held_at = (((orb_c ^ core) * 4 + (col - orb_x) % 4) * 8 + z_at).T.reshape(-1)
    o0, o1, o2, o3, occ = call(
        integral_kernel,
        [jnp.concatenate([rep1, held_at])],
        pieces,
        share_structs + [struct((32, 1, 128), F32)],
        [pltpu.VMEM((64, 144, 128), BF16), share_scratch],
        streamed=pair_rotations,
        limit=50 << 20,
    )

    energy_col = lax.dynamic_slice_in_dim(pair_energies[:, 1], rep * 32, 32, 1)
    energy = energy_col[:, :, None] + pair_energies[:, 0][:, None, :]
    ranks = jnp.concatenate([rep1, pair_ranks])
    other_slots = shift(send_slots, "pairs_2", 2, 1)
    slots = jnp.concatenate(
        [lax.dynamic_index_in_dim(s.reshape(32, 2, 2), core, 1) for s in (send_slots, other_slots)],
        1,
    ).reshape(-1)
    owner = couplings // 2
    arrived_at = (owner // 2) * 4 + ((owner % 2) ^ core) * 2 + couplings % 2
    links = jnp.concatenate([rep1, arrived_at.reshape(-1)])
    weights = coupling_weight.reshape(-1)

    occ, rep_late = lax.optimization_barrier((occ, rep1))
    turned, columns = call(
        columns_kernel,
        [rep_late],
        [],
        [struct((32, 6, 128, 128), BF16), struct((32, 128, 192), BF16)],
        [pltpu.VMEM((STEP, 192, 128), BF16)],
        streamed=margins,
        limit=42 << 20,
        cost=pl.CostEstimate(
            flops=32 * 6 * 2 * 128 * 128 * 192, bytes_accessed=9 << 20, transcendentals=0
        ),
    )
    integral, denominator, amplitude = call(
        start_kernel,
        [ranks],
        [*exchanged_over_rep((o0, o1, o2, o3)), energy, occ],
        [struct(share3, F32), struct(share3, F32), struct(share3, BF16)],
    )
    for turn in range(ITERS):
        (outgoing,) = call(
            outgoing_kernel,
            [slots],
            [amplitude, shift(amplitude, "pairs_2", 2, 1)],
            [struct((128, 32, 128), BF16)],
        )
        if turn == 0:
            outgoing, links, weights, turned, columns, ranks = lax.optimization_barrier(
                (outgoing, links, weights, turned, columns, ranks)
            )
        arrived = lax.all_to_all(outgoing, PLANE, 0, 0, tiled=True)
        shares = call(
            relax_kernel,
            [links, weights],
            [arrived, turned, columns],
            share_structs,
            [pltpu.VMEM((STEP, 192, 128), BF16), share_scratch],
        )
        (amplitude,) = call(
            update_kernel,
            [ranks],
            [*exchanged_over_rep(shares), integral, denominator],
            [struct(share3, BF16)],
        )

    parts = exchanged_over_rep([amplitude] * REP)
    dense_at = ((orb_c ^ core) * 32 + orb // 2).reshape(-1)
    final, d_own, d_other = call(
        density_kernel,
        [jnp.concatenate([rep1, dense_at])],
        parts,
        [struct((32, 128, 128), BF16), struct(share3, F32), struct(share3, F32)],
        [
            pltpu.VMEM((STEP, 128, 128), BF16),
            pltpu.VMEM((STEP, 256, 128), BF16),
            pltpu.VMEM((2 * STEP, 32, 128), F32),
            pltpu.VMEM((64, 32, 128), F32),
        ],
        streamed=pair_rotations,
        limit=12 << 20,
    )
    order = rep ^ jnp.arange(REP, dtype=jnp.int32)
    chosen = order[:, None] == jnp.arange(REP, dtype=jnp.int32)[None]
    chosen = jnp.broadcast_to(chosen.astype(F32)[:, :, None, None], (REP, REP, 1, 128))
    both = (d_own + shift(d_other, "pairs_2", 2, 1)).astype(BF16)
    both, chosen, final = lax.optimization_barrier((both, chosen, final))
    arrived = lax.all_to_all(both, PLANE, 0, 0, tiled=True)
    mine = jnp.sum(arrived.astype(F32), 0) / 128
    four = [mine] + [swap(mine, "rep", REP, k) for k in (2, 1, 3)]
    four = [four[0], four[2], four[1], four[3]]
    densities = sum(chosen[:, k] * four[k][None] for k in range(REP)).reshape(1, 128, 128)
    return (final, densities)


def solution(mesh):
    finer = Mesh(
        mesh.devices.reshape(8, 4, 2, mesh.shape["rep"]), ("pairs_0", "pairs_1", "pairs_2", "rep")
    )
    return jax.shard_map(
        body,
        mesh=finer,
        in_specs=(
            P(PAIRS, "rep", None),
            P(PAIRS, None, None),
            P(PAIRS),
            P(PAIRS, None, None, None),
            P(PAIRS, None, None),
            P(PAIRS, None),
            P(PAIRS),
            P(PAIRS, None, None, None),
            P(PAIRS, None),
            P(PAIRS, None, None),
            P(PAIRS, None),
        ),
        out_specs=(P(PAIRS, None, None), P(PAIRS, None, None)),
        check_vma=False,
    )
```

```python
import jax
import jax.numpy as jnp
from jax import lax
from jax.experimental import pallas as pl
from jax.experimental.pallas import tpu as pltpu
from jax.sharding import Mesh
from jax.sharding import PartitionSpec as P

ITERS = 3
PAIRS = ("pairs_0", "pairs_1", "pairs_2")
PLANE = ("pairs_1", "pairs_0")
REP = 4
STEP = 8
LIMIT = 12 << 20
F32, BF16 = jnp.float32, jnp.bfloat16
NN = (((1,), (0,)), ((), ()))
NT = (((1,), (1,)), ((), ()))
TN = (((0,), (0,)), ((), ()))


def mm(a, b, dims):
    return lax.dot_general(a, b, dims, preferred_element_type=F32)


def shift(x, axis, count, by):
    return lax.ppermute(x, axis, [(i, (i + by) % count) for i in range(count)])


def swap(x, axis, count, bit):
    return lax.ppermute(x, axis, [(i, i ^ bit) for i in range(count)])


def store_shares(share_ref, n, rank_at, outs, at):
    for k, out in enumerate(outs):
        first = pl.multiple_of(lax.rem(rank_at + k, REP) * 32, 32)
        out[at] = share_ref[n, pl.ds(first, 32), :].astype(out.dtype)


def each_step(body_of):
    def one(step, carry):
        body_of(step)
        return carry

    lax.fori_loop(0, 32 // STEP, one, 0)


def integral_kernel(idx, *refs):
    pieces, (rot, o0, o1, o2, o3, occ, held, share) = refs[:16], refs[16:]
    step = pl.program_id(0)

    @pl.when(step == 0)
    def _():
        for i, piece in enumerate(pieces):
            first = i % 8 * 8 + i // 8 * 4
            held[first : first + 4] = piece[...]

    halves = []
    for n in range(STEP):
        p = step * STEP + n
        left = mm(held[idx[1 + p], :128, :], rot[n, 0], NN)
        right = mm(held[idx[33 + p], :128, :], rot[n, 1], NN)
        left_hi, right_hi = left.astype(BF16), right.astype(BF16)
        left_lo = (left - left_hi.astype(F32)).astype(BF16)
        right_lo = (right - right_hi.astype(F32)).astype(BF16)
        halves.append((right_hi, right_lo, left_hi, left_lo))
    for n in range(STEP):
        right_hi, right_lo, left_hi, left_lo = halves[n]
        four = mm(
            jnp.concatenate([right_hi, right_lo], 1), jnp.concatenate([left_hi, left_lo], 1), TN
        )
        share[n] = four[:128, :128] + four[:128, 128:] + four[128:, :128]
    for n in range(STEP):
        p = step * STEP + n
        i, j = idx[1 + p], idx[33 + p]
        store_shares(share, n, idx[0], (o0, o1, o2, o3), p)
        occ[p] = held[i, 128:144, :].astype(F32)[:1] + held[j, 128:144, :].astype(F32)[:1]


def visible_rows(idx, p, first):
    rank = idx[1 + p]
    b = lax.broadcasted_iota(jnp.int32, (32, 128), 0) + first
    a = lax.broadcasted_iota(jnp.int32, (32, 128), 1)
    return (b < rank) & (a < rank)


def start_kernel(idx, own, r1, r2, r3, energy, occ, integral, denominator, amplitude):
    first = idx[0] * 32

    def one(p, carry):
        total = own[p] + r1[p].astype(F32) + r2[p].astype(F32) + r3[p].astype(F32)
        value = jnp.where(visible_rows(idx, p, first), total, 0.0)
        denom = energy[p] - occ[p]
        integral[p] = value
        denominator[p] = denom
        amplitude[p] = (-value / denom).astype(BF16)
        return carry

    lax.fori_loop(0, 32, one, 0, unroll=4)


def update_kernel(idx, own, r1, r2, r3, integral, denominator, amplitude):
    first = idx[0] * 32

    def one(p, carry):
        coupled = own[p] + r1[p].astype(F32) + r2[p].astype(F32) + r3[p].astype(F32)
        value = -(integral[p] - coupled) / denominator[p]
        amplitude[p] = jnp.where(visible_rows(idx, p, first), value, 0.0).astype(BF16)
        return carry

    lax.fori_loop(0, 32, one, 0, unroll=4)


def outgoing_kernel(idx, own, other, out):
    def one(d, carry):
        for s in range(2):
            out[d * 4 + s] = own[idx[d * 4 + s]]
            out[d * 4 + 2 + s] = other[idx[d * 4 + 2 + s]]
        return carry

    lax.fori_loop(0, 32, one, 0, unroll=4)


def columns_kernel(idx, margin, turned, out, rows):
    step, mine = pl.program_id(0), pl.multiple_of(idx[0] * 32, 32)
    for n in range(STEP):
        for c in range(6):
            turned[step * STEP + n, c] = margin[n, c].T
    for n in range(STEP):
        for c in range(6):
            rows[n, 32 * c : 32 * c + 32, :] = turned[step * STEP + n, c, pl.ds(mine, 32), :]
    for n in range(STEP):
        out[step * STEP + n] = rows[n].T


def relax_kernel(idx, weight, arrived, turned, columns, o0, o1, o2, o3, lefts, share):
    def some(step):
        for n in range(STEP):
            p = step * STEP + n
            for c in range(6):
                left = mm(arrived[idx[1 + p * 6 + c]], turned[p, c], NN)
                lefts[n, 32 * c : 32 * c + 32, :] = (left * weight[p * 6 + c]).astype(BF16)
        for n in range(STEP):
            share[n] = mm(columns[step * STEP + n], lefts[n], NN)
        for n in range(STEP):
            store_shares(share, n, idx[0], (o0, o1, o2, o3), step * STEP + n)

    each_step(some)


def density_kernel(idx, t0, t1, t2, t3, rot, amplitude, d0, d1, whole, sides, grams, acc):
    step, mine = pl.program_id(0), pl.multiple_of(idx[0] * 32, 32)

    @pl.when(step == 0)
    def _():
        acc[...] = jnp.zeros_like(acc)

    for n in range(STEP):
        for k, piece in enumerate((t0, t1, t2, t3)):
            first = pl.multiple_of(lax.rem(idx[0] + REP - k, REP) * 32, 32)
            whole[n, pl.ds(first, 32), :] = piece[step * STEP + n]
    for n in range(STEP):
        p = step * STEP + n
        amp_t = whole[n]
        amplitude[p] = amp_t.T
        sides[n, :128] = mm(rot[n, 0], amp_t, NT).astype(BF16)
        sides[n, 128:] = mm(rot[n, 1], amp_t, NN).astype(BF16)
    for n in range(STEP):
        rows = [sides[n, pl.ds(mine + at, 32), :] for at in (0, 128)]
        both = mm(jnp.concatenate(rows, 0), sides[n], NT)
        grams[2 * n] = both[:32, :128]
        grams[2 * n + 1] = both[32:, 128:]

    def add(k, carry):
        at = idx[1 + step * 2 * STEP + k]
        acc[at] = acc[at] + grams[k]
        return carry

    lax.fori_loop(0, 2 * STEP, add, 0)

    @pl.when(step == pl.num_programs(0) - 1)
    def _():
        d0[...] = acc[:32]
        d1[...] = acc[32:]


def call(kernel, scalars, args, outs, scratch=(), cost=None, streamed=None, limit=LIMIT):
    vmem, smem = pl.BlockSpec(memory_space=pltpu.VMEM), pl.BlockSpec(memory_space=pltpu.SMEM)
    specs, grid = [smem] * len(scalars) + [vmem] * len(args), ()
    if streamed is not None:
        block = (STEP, *streamed.shape[1:])
        specs.append(pl.BlockSpec(block, lambda g: (g,) + (0,) * (len(block) - 1)))
        args, grid = [*args, streamed], (32 // STEP,)
    return pl.pallas_call(
        kernel,
        grid=grid,
        in_specs=specs,
        out_specs=[vmem] * len(outs),
        scratch_shapes=list(scratch),
        out_shape=outs,
        cost_estimate=cost,
        compiler_params=pltpu.CompilerParams(vmem_limit_bytes=limit),
    )(*scalars, *args)


def struct(shape, dtype):
    return jax.ShapeDtypeStruct(shape, dtype)


def exchanged_over_rep(shares):
    far = {k: shift(shares[k], "rep", REP, k) for k in (2, 1, 3)}
    return shares[0], far[1], far[2], far[3]


def body(
    factors,
    orbital_virtuals,
    occupied,
    pair_rotations,
    pair_energies,
    pair_orbitals,
    pair_ranks,
    margins,
    coupling_weight,
    send_slots,
    couplings,
):
    core, rep, col = lax.axis_index("pairs_2"), lax.axis_index("rep"), lax.axis_index("pairs_1")
    rep1 = rep[None].astype(jnp.int32)
    share3 = (32, 32, 128)
    share_structs = [struct(share3, F32)] + [struct(share3, BF16)] * 3
    share_scratch = pltpu.VMEM((STEP, 128, 128), F32)

    halves = mm(factors[0], orbital_virtuals[0], NN).astype(BF16)
    sent = jnp.concatenate([halves, jnp.broadcast_to(occupied[:, None], (16, 128))], 0)
    near = sent[None]
    for bit in (4, 2):
        near = jnp.concatenate([near, swap(near, "pairs_0", 8, bit)], 0)
    pieces = []
    for group in (near, swap(near, "pairs_0", 8, 1)):
        along_x = [group] + [shift(group, "pairs_1", 4, k) for k in (1, 2, 3)]
        pieces += along_x + [shift(piece, "pairs_2", 2, 1) for piece in along_x]

    orb = pair_orbitals
    orb_z, orb_x, orb_c = orb // 8, (orb // 2) % 4, orb % 2
    apart = orb_z ^ lax.axis_index("pairs_0")
    z_at = (apart // 4) + (apart // 2) % 2 * 2 + apart % 2 * 4
    held_at = (((orb_c ^ core) * 4 + (col - orb_x) % 4) * 8 + z_at).T.reshape(-1)
    o0, o1, o2, o3, occ = call(
        integral_kernel,
        [jnp.concatenate([rep1, held_at])],
        pieces,
        share_structs + [struct((32, 1, 128), F32)],
        [pltpu.VMEM((64, 144, 128), BF16), share_scratch],
        streamed=pair_rotations,
        limit=50 << 20,
    )

    energy_col = lax.dynamic_slice_in_dim(pair_energies[:, 1], rep * 32, 32, 1)
    energy = energy_col[:, :, None] + pair_energies[:, 0][:, None, :]
    ranks = jnp.concatenate([rep1, pair_ranks])
    other_slots = shift(send_slots, "pairs_2", 2, 1)
    slots = jnp.concatenate(
        [
            lax.dynamic_index_in_dim(s.reshape(8, 4, 2, 2), core, 2).swapaxes(0, 1).reshape(32, 1, 2)
            for s in (send_slots, other_slots)
        ],
        1,
    ).reshape(-1)
    owner = couplings // 2
    plane_at = (owner // 2) % 4 * 8 + owner // 8
    arrived_at = plane_at * 4 + ((owner % 2) ^ core) * 2 + couplings % 2
    links = jnp.concatenate([rep1, arrived_at.reshape(-1)])
    weights = coupling_weight.reshape(-1)

    occ, rep_late = lax.optimization_barrier((occ, rep1))
    turned, columns = call(
        columns_kernel,
        [rep_late],
        [],
        [struct((32, 6, 128, 128), BF16), struct((32, 128, 192), BF16)],
        [pltpu.VMEM((STEP, 192, 128), BF16)],
        streamed=margins,
        limit=42 << 20,
        cost=pl.CostEstimate(
            flops=32 * 6 * 2 * 128 * 128 * 192, bytes_accessed=9 << 20, transcendentals=0
        ),
    )
    integral, denominator, amplitude = call(
        start_kernel,
        [ranks],
        [*exchanged_over_rep((o0, o1, o2, o3)), energy, occ],
        [struct(share3, F32), struct(share3, F32), struct(share3, BF16)],
    )
    for turn in range(ITERS):
        (outgoing,) = call(
            outgoing_kernel,
            [slots],
            [amplitude, shift(amplitude, "pairs_2", 2, 1)],
            [struct((128, 32, 128), BF16)],
        )
        if turn == 0:
            outgoing, links, weights, turned, columns, ranks = lax.optimization_barrier(
                (outgoing, links, weights, turned, columns, ranks)
            )
        arrived = lax.all_to_all(outgoing, PLANE, 0, 0, tiled=True)
        shares = call(
            relax_kernel,
            [links, weights],
            [arrived, turned, columns],
            share_structs,
            [pltpu.VMEM((STEP, 192, 128), BF16), share_scratch],
        )
        (amplitude,) = call(
            update_kernel,
            [ranks],
            [*exchanged_over_rep(shares), integral, denominator],
            [struct(share3, BF16)],
        )

    parts = exchanged_over_rep([amplitude] * REP)
    dense_at = ((orb_c ^ core) * 32 + orb_x * 8 + orb_z).reshape(-1)
    final, d_own, d_other = call(
        density_kernel,
        [jnp.concatenate([rep1, dense_at])],
        parts,
        [struct((32, 128, 128), BF16), struct(share3, F32), struct(share3, F32)],
        [
            pltpu.VMEM((STEP, 128, 128), BF16),
            pltpu.VMEM((STEP, 256, 128), BF16),
            pltpu.VMEM((2 * STEP, 32, 128), F32),
            pltpu.VMEM((64, 32, 128), F32),
        ],
        streamed=pair_rotations,
        limit=12 << 20,
    )
    order = rep ^ jnp.arange(REP, dtype=jnp.int32)
    chosen = order[:, None] == jnp.arange(REP, dtype=jnp.int32)[None]
    chosen = jnp.broadcast_to(chosen.astype(F32)[:, :, None, None], (REP, REP, 1, 128))
    both = (d_own + shift(d_other, "pairs_2", 2, 1)).astype(BF16)
    both, chosen, final = lax.optimization_barrier((both, chosen, final))
    arrived = lax.all_to_all(both, PLANE, 0, 0, tiled=True)
    mine = jnp.sum(arrived.astype(F32), 0) / 128
    four = [mine] + [swap(mine, "rep", REP, k) for k in (2, 1, 3)]
    four = [four[0], four[2], four[1], four[3]]
    densities = sum(chosen[:, k] * four[k][None] for k in range(REP)).reshape(1, 128, 128)
    return (final, densities)


def solution(mesh):
    finer = Mesh(
        mesh.devices.reshape(8, 4, 2, mesh.shape["rep"]), ("pairs_0", "pairs_1", "pairs_2", "rep")
    )
    return jax.shard_map(
        body,
        mesh=finer,
        in_specs=(
            P(PAIRS, "rep", None),
            P(PAIRS, None, None),
            P(PAIRS),
            P(PAIRS, None, None, None),
            P(PAIRS, None, None),
            P(PAIRS, None),
            P(PAIRS),
            P(PAIRS, None, None, None),
            P(PAIRS, None),
            P(PAIRS, None, None),
            P(PAIRS, None),
        ),
        out_specs=(P(PAIRS, None, None), P(PAIRS, None, None)),
        check_vma=False,
    )
```
